128 devices in a mesh: nodes: 32 (over z, y_hi, x), grid: 4 (over y_lo, core).
Axes of the slice: x: 4, y: 4 (y_hi: 2, y_lo: 2; y = y_hi * 2 + y_lo), z: 4, core: 2. Of those that a mesh axis runs over, the one named last changes fastest.
Arguments:
- block: float32 [256, 262144], P('grid', 'nodes')
- inv_sqrt_mass: float32 [262144], P('nodes'), may hold values from 0.6 to 1.6
- potential: float32 [262144], P('nodes'), may hold values from -2 to 1
- elem_scale: float32 [4096], P('nodes'), may hold values from 0.5 to 2
- connectivity: int32 [4096, 125], P('nodes'), may hold values from 0 to 10239, as said below
- elem_matrix: float32 [125, 125], replicated, as said below
Outputs:
- filtered_cyclic: float32 [256, 262144], P('grid', 'nodes')
- intersection: float32 [256, 256], P(None, 'grid')
The draws below stay inside these ranges and needn't reach their ends.
Inputs may be any that keep to these rules, and one draw needn't show every extreme that they name: `connectivity`: each row is an element of partition p = row // 128; its entries number the partition's 8192 own nodes from 0, then from 8192 the first 2048 nodes of the next partition. Element j of a partition uses nodes j * 64 to j * 64 + 2111; entries may repeat within an element. `elem_matrix`: Symmetric, with diagonal entries about 3 plus a full off-diagonal part.
All inputs are finite; a program needn't handle non-finite values.
Results may differ from the reference program's by a relative error of at most 0.0003.
Values sent between devices are 32-bit elements; how exact they have to be, the bound alone decides.
No kernel may reach another device: no remote copies, remote signals or barrier semaphores. Data moves between devices by JAX's collectives and lax.ppermute only.
A program may use at most 64 MiB of HBM per device.

```python
import math
import jax
import jax.numpy as jnp
from jax import lax

BLOCK = 256
NPE = 125
ND = 8192
NODE_STRIDE = 64
RIM = 2048
NB = 128
SB = 16
E_DEV = 128
NODES = 262144
ELEMS = 4096
N_NODES = 32
N_GRID = 4


def draw_block(key, part):
    position = jnp.arange(NODES).astype(jnp.float32)
    rising = 1.0 + 2.0 * position / (NODES - 1)
    mix_key = jax.random.fold_in(key, 11)
    field_key = jax.random.fold_in(key, 23)
    noise_key = jax.random.fold_in(key, 37)
    mixing = jax.random.normal(mix_key, (BLOCK, 8), jnp.float32) * 8.0 ** (-0.5)
    fields = jax.random.normal(field_key, (8, NODES), jnp.float32)
    noise = jax.random.normal(noise_key, (BLOCK, NODES), jnp.float32)
    values = 0.7 * noise
    for common in range(8):
        values = values + mixing[:, common:common + 1] * fields[common][None, :]
    return values * rising[None, :]


def draw_connectivity(key, part):
    window = NODE_STRIDE + RIM
    offsets = jax.random.randint(key, (ELEMS, NPE), 0, window)
    offsets = offsets.at[:, 0].set(0).at[:, NPE - 1].set(window - 1)
    element = jnp.arange(ELEMS) % E_DEV
    return (element[:, None] * NODE_STRIDE + offsets).astype(jnp.int32)


def draw_elem_matrix(key, part):
    noise = jax.random.normal(key, (NPE, NPE), jnp.float32)
    return 0.03 * (noise + noise.T) + 3.0 * jnp.eye(NPE, dtype=jnp.float32)


def block_levels(rng, dims, split, smallest, top_value):
    loudness = 1.0
    for axis_at, parts in split:
        steps = jax.random.uniform(jax.random.fold_in(jax.random.fold_in(rng, 6), axis_at), (parts,), jnp.float32, smallest / len(split), top_value / len(split))
        loudness = loudness * jnp.repeat(jnp.exp(steps), dims[axis_at] // parts).reshape((-1,) + (1,) * (len(dims) - 1 - axis_at))
    return loudness


def setup_inputs(seed: int = 0) -> dict:
    streams_of = jax.random.split(jax.random.key(seed), 7)
    block = draw_block(jax.random.fold_in(streams_of[6], 71), 0)
    inv_sqrt_mass = jnp.clip(jnp.exp(math.log(1.6) - 0.98082923 * jax.random.uniform(streams_of[1], (NODES,), jnp.float32) ** block_levels(streams_of[1], (NODES,), ((0, 32),), -0.2, 0.2)), 0.6, 1.6)
    potential = jnp.clip(-2.0 + 3.0 * jax.random.uniform(streams_of[2], (NODES,), jnp.float32) ** block_levels(streams_of[2], (NODES,), ((0, 32),), -0.2, 0.2), -2.0, 1.0)
    elem_scale = jnp.clip(jnp.exp(math.log(2.0) - 1.3862944 * jax.random.uniform(streams_of[3], (ELEMS,), jnp.float32) ** block_levels(streams_of[3], (ELEMS,), ((0, 32),), -0.2, 0.2)), 0.5, 2.0)
    connectivity = draw_connectivity(jax.random.fold_in(streams_of[6], 71), 0)
    elem_matrix = draw_elem_matrix(jax.random.fold_in(streams_of[6], 71), 0)
    return dict(block=block, inv_sqrt_mass=inv_sqrt_mass, potential=potential, elem_scale=elem_scale, connectivity=connectivity, elem_matrix=elem_matrix)


def apply_operator(field, inv_sqrt_mass, potential, scale_parts, conn_parts, elem_matrix):
    scaled = inv_sqrt_mass[None, :] * field
    wide = jnp.concatenate([scaled, jnp.zeros((BLOCK, RIM), jnp.float32)], axis=1)
    starts = (jnp.arange(N_NODES) * ND).astype(jnp.int32)

    def add_part(total, item):
        part_conn, part_scale, start = item
        global_nodes = (part_conn.T + start).astype(jnp.int32)
        picked = wide[:, global_nodes]
        local = jnp.einsum('ab,sbe->sae', elem_matrix, picked, precision=lax.Precision.HIGHEST)
        local = local * part_scale[None, None, :]
        return (total.at[:, global_nodes].add(local), None)
    summed, unused = lax.scan(add_part, jnp.zeros((BLOCK, NODES + RIM), jnp.float32), (conn_parts, scale_parts, starts))
    return inv_sqrt_mass[None, :] * summed[:, :NODES] + potential[None, :] * field

def reference(block, inv_sqrt_mass, potential, elem_scale, connectivity, elem_matrix):
    conn_parts = connectivity.reshape(N_NODES, E_DEV, NPE)
    scale_parts = elem_scale.reshape(N_NODES, E_DEV)
    lowest, cut, top = (-2.0, 4.0, 32.0)
    half = (top - cut) / 2.0
    centre = (top + cut) / 2.0
    sigma = half / (lowest - centre)
    sigma_two = 1.0 / (2.0 / sigma - sigma)
    image = apply_operator(block, inv_sqrt_mass, potential, scale_parts, conn_parts, elem_matrix)
    first = sigma / half * (image - centre * block)
    image_two = apply_operator(first, inv_sqrt_mass, potential, scale_parts, conn_parts, elem_matrix)
    filtered = 2.0 * (sigma_two / half) * (image_two - centre * first) - sigma * sigma_two * block
    blocks = NODES // (N_NODES * NB)
    shaped = filtered.reshape(N_GRID, N_GRID, SB, blocks, N_NODES, NB)
    cyclic = shaped.transpose(1, 0, 2, 4, 3, 5).reshape(BLOCK, NODES)
    intersection = jnp.dot(cyclic, cyclic.T, precision=lax.Precision.HIGHEST) / NODES
    return (cyclic, intersection)
```

```python
import functools

import jax
import jax.numpy as jnp
from jax import lax
from jax.experimental import pallas as pl
from jax.experimental.pallas import tpu as pltpu
from jax.sharding import PartitionSpec as P

F32, BF16 = jnp.float32, jnp.bfloat16
HB = 2048
LANES = 128
NPE = 125
EL = 32
GROUP = 8
NB, SB = 128, 16

LOWEST, CUT, TOP = -2.0, 4.0, 32.0
HALF = (TOP - CUT) / 2.0
CENTRE = (TOP + CUT) / 2.0
SIGMA = HALF / (LOWEST - CENTRE)
SIGMA_TWO = 1.0 / (2.0 / SIGMA - SIGMA)
A1 = SIGMA / HALF
A2 = 2.0 * SIGMA_TWO / HALF
A3 = SIGMA * SIGMA_TWO

VM = pl.BlockSpec(memory_space=pltpu.VMEM)
SM = pl.BlockSpec(memory_space=pltpu.SMEM)
NODE_BLOCK = jax.ShapeDtypeStruct((HB, LANES), F32)


def split(value):
    high = value.astype(BF16)
    return high, (value - high.astype(F32)).astype(BF16)


def dot(a, b):
    return lax.dot_general(a, b, (((1,), (0,)), ((), ())), preferred_element_type=F32)


def dot_t(a, b):
    return lax.dot_general(a, b, (((1,), (1,)), ((), ())), preferred_element_type=F32)


def cost(microseconds):
    return pl.CostEstimate(flops=0, transcendentals=0, bytes_accessed=int(microseconds * 3.0e6))


def add_elements(conn, scale, matrix, values, picked, local, sums):
    high, low = split(matrix[...])
    for ref in picked:
        ref[pl.ds(NPE, LANES - NPE), :] = jnp.zeros((LANES - NPE, LANES), F32)
    for ref in sums:
        ref[...] = jnp.zeros_like(ref)

    @pl.loop(0, EL // GROUP)
    def _(step):
        for i in range(NPE):
            for k in range(GROUP):
                node = conn[step * (GROUP * LANES) + k * LANES + i]
                picked[k][pl.ds(i, 1), :] = values[pl.ds(node, 1), :]
        for k in range(GROUP):
            p_high, p_low = split(picked[k][...])
            product = dot(high, p_high) + (dot(low, p_high) + dot(high, p_low))
            local[k][...] = product * scale[step * GROUP + k]
        for i in range(NPE):
            for k in range(GROUP):
                node = conn[step * (GROUP * LANES) + k * LANES + i]
                row = pl.ds(node, 1)
                sums[k][row, :] = sums[k][row, :] + local[k][pl.ds(i, 1), :]


def store_sums(sums, low_ref, high_ref):
    for target, start in ((low_ref, 0), (high_ref, HB)):
        part = pl.ds(start, HB)
        parts = [ref[part, :] for ref in sums]
        while len(parts) > 1:
            parts = [a + b for a, b in zip(parts[::2], parts[1::2])]
        target[...] = parts[0]


def first_kernel(conn, scale, matrix, v0, v1, m0, m1, low_ref, high_ref, values, *scratch):
    picked, local, sums = scratch[:GROUP], scratch[GROUP:2 * GROUP], scratch[2 * GROUP:]
    values[pl.ds(0, HB), :] = v0[...] * m0[...]
    values[pl.ds(HB, HB), :] = v1[...] * m1[...]
    add_elements(conn, scale, matrix, values, picked, local, sums)
    store_sums(sums, low_ref, high_ref)


def upper_kernel(conn, scale, matrix, a0, b0, a1, b1, v0, v1, m0, m1, w0, w1,
                 low_ref, high_ref, x0_ref, values, *scratch):
    picked, local, sums = scratch[:GROUP], scratch[GROUP:2 * GROUP], scratch[2 * GROUP:]
    x0 = A1 * (m0[...] * (a0[...] + b0[...]) + w0[...] * v0[...])
    x0_ref[...] = x0
    values[pl.ds(0, HB), :] = m0[...] * x0
    x1 = A1 * (m1[...] * (a1[...] + b1[...]) + w1[...] * v1[...])
    values[pl.ds(HB, HB), :] = m1[...] * x1
    add_elements(conn, scale, matrix, values, picked, local, sums)
    store_sums(sums, low_ref, high_ref)


def lower_kernel(conn, scale, matrix, a0, b0, v0, x1, m0, m1, w0,
                 low_ref, high_ref, x0_ref, values, *scratch):
    picked, local, sums = scratch[:GROUP], scratch[GROUP:2 * GROUP], scratch[2 * GROUP:]
    x0 = A1 * (m0[...] * (a0[...] + b0[...]) + w0[...] * v0[...])
    x0_ref[...] = x0
    values[pl.ds(0, HB), :] = m0[...] * x0
    values[pl.ds(HB, HB), :] = m1[...] * x1[...]
    add_elements(conn, scale, matrix, values, picked, local, sums)
    store_sums(sums, low_ref, high_ref)


def element_call(kernel, outs, *operands):
    return pl.pallas_call(
        kernel,
        out_shape=(NODE_BLOCK,) * outs,
        in_specs=[SM, SM] + [VM] * (len(operands) - 2),
        out_specs=(VM,) * outs,
        scratch_shapes=[pltpu.VMEM((2 * HB, LANES), F32)]
        + [pltpu.VMEM((LANES, LANES), F32)] * (2 * GROUP)
        + [pltpu.VMEM((2 * HB, LANES), F32)] * GROUP,
        compiler_params=pltpu.CompilerParams(vmem_limit_bytes=48 << 20),
        cost_estimate=cost(14),
    )(*operands)


def spread_kernel(mass, well, mass_ref, well_ref):
    for chunk in range(mass.shape[0]):
        rows = pl.ds(chunk * LANES, LANES)
        one = jnp.broadcast_to(mass[pl.ds(chunk, 1), :], (LANES, LANES))
        mass_ref[rows, :] = one.T
        two = jnp.broadcast_to(well[pl.ds(chunk, 1), :] - CENTRE, (LANES, LANES))
        well_ref[rows, :] = two.T


def spread(mass, well):
    out = jax.ShapeDtypeStruct((mass.shape[0] * LANES, LANES), F32)
    return pl.pallas_call(
        spread_kernel,
        out_shape=(out, out),
        in_specs=[VM, VM],
        out_specs=(VM, VM),
        cost_estimate=cost(3),
    )(mass, well)


CHUNK = 512


def enter_kernel(core, mine, other, low_ref, high_ref):
    step = pl.program_id(0)
    for part in range(CHUNK // LANES):
        columns = pl.ds(part * LANES, LANES)
        a, b = mine[:, columns], other[:, columns]
        first = core[0] == 0
        stacked = jnp.concatenate([jnp.where(first, a, b), jnp.where(first, b, a)], axis=0)
        turned = stacked.T
        rows = pl.ds(pl.multiple_of((step % (HB // CHUNK)) * CHUNK + part * LANES, LANES), LANES)

        @pl.when(step < HB // CHUNK)
        def _():
            low_ref[rows, :] = turned

        @pl.when(step >= HB // CHUNK)
        def _():
            high_ref[rows, :] = turned


def enter(core, block, other):
    states = block.shape[0]
    steps = 2 * HB // CHUNK
    whole = pl.BlockSpec((HB, LANES), lambda i, c: (0, 0))
    return pl.pallas_call(
        enter_kernel,
        out_shape=(NODE_BLOCK, NODE_BLOCK),
        grid_spec=pltpu.PrefetchScalarGridSpec(
            num_scalar_prefetch=1,
            grid=(steps,),
            in_specs=[
                pl.BlockSpec((states, CHUNK), lambda i, c: (0, c[0] * steps + i)),
                pl.BlockSpec((states, CHUNK), lambda i, c: (0, i)),
            ],
            out_specs=(whole, whole),
        ),
        cost_estimate=cost(3),
    )(core, block, other)


def finish_kernel(lo_d, hi_c, hi_d, lo_c, v_l, v_u, x_l, x_u, m_l, m_u, w_l, w_u, out_ref):
    halves = (
        (lo_d, hi_c, v_l, x_l, m_l, w_l),
        (hi_d, lo_c, v_u, x_u, m_u, w_u),
    )
    count = HB // LANES
    for half, (a, b, v, x, m, w) in enumerate(halves):
        for chunk in range(count):
            rows = pl.ds(chunk * LANES, LANES)
            value = A2 * (m[rows, :] * (a[rows, :] + b[rows, :]) + w[rows, :] * x[rows, :])
            turned = (value - A3 * v[rows, :]).T
            for kk in range(2):
                for c in range(4):
                    source = kk * 64 + c * SB
                    out_ref[half * count + chunk, pl.ds(c * 2 * SB + kk * SB, SB), :] = turned[
                        source:source + SB, :
                    ]


def finish(*operands):
    return pl.pallas_call(
        finish_kernel,
        out_shape=jax.ShapeDtypeStruct((2 * HB // LANES, LANES, LANES), F32),
        in_specs=[VM] * len(operands),
        out_specs=VM,
        compiler_params=pltpu.CompilerParams(vmem_limit_bytes=40 << 20),
        cost_estimate=cost(4),
    )(*operands)


def overlap_kernel(weight, row, mine, other, out_ref, main, cross):
    main[...] = jnp.zeros_like(main)
    cross[...] = jnp.zeros_like(cross)
    first = row[0] == 0

    @pl.loop(0, mine.shape[0] // 2)
    def _(step):
        blocks = []
        for c in range(4):
            rows = pl.ds(c * 2 * SB, 2 * SB)
            a = jnp.concatenate([mine[2 * step, rows, :], mine[2 * step + 1, rows, :]], axis=1)
            b = jnp.concatenate([other[2 * step, rows, :], other[2 * step + 1, rows, :]], axis=1)
            blocks += [jnp.where(first, a, b), jnp.where(first, b, a)]
        high, low = split(jnp.concatenate(blocks, axis=0))
        main[...] += dot_t(high, high)
        cross[...] += dot_t(high, low)

    out_ref[...] = (main[...] + (cross[...] + cross[...].T)) * weight


def overlap(weight, row, mine, other):
    states = 2 * LANES
    return pl.pallas_call(
        functools.partial(overlap_kernel, weight),
        out_shape=jax.ShapeDtypeStruct((states, states), F32),
        in_specs=[SM, VM, VM],
        out_specs=VM,
        scratch_shapes=[pltpu.VMEM((states, states), F32)] * 2,
        cost_estimate=cost(4),
    )(row, mine, other)


def shards(block, inv_sqrt_mass, potential, elem_scale, connectivity, elem_matrix):
    both = ("nodes", "grid")
    parts = lax.axis_size("nodes")
    grid = lax.axis_index("grid")
    row, core = grid // 2, grid % 2
    owned = 2 * HB

    def along(step):
        pairs = []
        for y in range(2):
            for source in range(2 * parts):
                target = source + step
                if 0 <= target < 2 * parts:
                    pairs.append((
                        source // 2 * 4 + y * 2 + source % 2,
                        target // 2 * 4 + y * 2 + target % 2,
                    ))
        return lambda value: lax.ppermute(value, both, pairs)

    to_previous, to_next = along(-1), along(1)

    other = lax.dynamic_slice(block, (0, (1 - core) * owned), (block.shape[0], owned))
    other = lax.ppermute(other, "grid", [(0, 1), (1, 0), (2, 3), (3, 2)])
    fields = jnp.stack([inv_sqrt_mass, potential])
    rim = lax.ppermute(fields[:, :HB], "nodes", [(n, n - 1) for n in range(1, parts)])
    own_fields = lax.dynamic_slice(fields, (0, core * owned), (2, owned))
    last = jnp.where(core == 0, fields[:, owned:owned + HB], rim)
    fields = jnp.concatenate([own_fields, last], axis=1).reshape(2, 3 * HB // LANES, LANES)
    mass, well = spread(fields[0], fields[1])
    m_l, m_u, m_h = mass[:HB], mass[HB:2 * HB], mass[2 * HB:]
    w_l, w_u, w_h = well[:HB], well[HB:2 * HB], well[2 * HB:]

    conn = lax.dynamic_slice(connectivity, (core * 2 * EL, 0), (2 * EL, NPE)) - core * owned
    conn = jnp.pad(conn, ((0, 0), (0, LANES - NPE)))
    c_l, c_u = conn[:EL].reshape(-1), (conn[EL:] - HB).reshape(-1)
    scale = lax.dynamic_slice(elem_scale, (core * 2 * EL,), (2 * EL,))
    s_l, s_u = scale[:EL], scale[EL:]
    matrix = jnp.pad(elem_matrix, ((0, LANES - NPE), (0, LANES - NPE)))

    v_l, v_u = enter(core[None], block, other)
    v_h = to_previous(v_l)
    lo_a, hi_a = element_call(first_kernel, 2, c_l, s_l, matrix, v_l, v_u, m_l, m_u)
    lo_a_next = to_previous(lo_a)
    lo_b, hi_b = element_call(first_kernel, 2, c_u, s_u, matrix, v_u, v_h, m_u, m_h)
    hi_b_previous = to_next(hi_b)
    lo_c, hi_c, x_u = element_call(
        upper_kernel, 3, c_u, s_u, matrix,
        hi_a, lo_b, hi_b, lo_a_next, v_u, v_h, m_u, m_h, w_u, w_h,
    )
    hi_c_previous = to_next(hi_c)
    lo_d, hi_d, x_l = element_call(
        lower_kernel, 3, c_l, s_l, matrix,
        lo_a, hi_b_previous, v_l, x_u, m_l, m_u, w_l,
    )
    tiles = finish(lo_d, hi_c_previous, hi_d, lo_c, v_l, v_u, x_l, x_u, m_l, m_u, w_l, w_u)

    count = HB // LANES
    away = lax.dynamic_slice(tiles, ((1 - row) * count, 0, 0), (count, LANES, LANES))
    kept = lax.dynamic_slice(tiles, (row * count, 0, 0), (count, LANES, LANES))
    received = lax.ppermute(away, "grid", [(0, 2), (1, 3), (2, 0), (3, 1)])

    moved = lax.all_to_all(
        tiles.reshape(4 * parts, 2 * SB, NB), both, split_axis=0, concat_axis=0, tiled=True
    )
    cyclic = moved.reshape(parts, 2, 2, 2 * SB, NB).transpose(1, 3, 0, 2, 4)
    cyclic = cyclic.reshape(block.shape)

    weight = 1.0 / (parts * 4 * HB)
    panel = overlap(weight, row[None], kept, received)
    states = panel.shape[0]
    shares = panel.reshape(4, parts, states // (4 * parts) * 2, LANES).transpose(1, 0, 2, 3)
    shares = shares.reshape(4 * parts, -1, LANES)
    shares = lax.all_to_all(shares, both, split_axis=0, concat_axis=0, tiled=True)
    total = jnp.sum(shares, axis=0)
    rows = lax.all_to_all(
        jnp.broadcast_to(total[None], (parts,) + total.shape),
        "nodes", split_axis=0, concat_axis=0, tiled=True,
    )
    intersection = rows.reshape(states // 4, states).T
    return (cyclic, intersection)


def solution(mesh):
    placed = (P("grid", "nodes"), P("nodes"), P("nodes"), P("nodes"), P("nodes", None), P())
    return jax.shard_map(
        shards,
        mesh=mesh,
        in_specs=placed,
        out_specs=(P("grid", "nodes"), P(None, "grid")),
        check_vma=False,
    )
```

```python
import functools

import jax
import jax.numpy as jnp
from jax import lax
from jax.experimental import pallas as pl
from jax.experimental.pallas import tpu as pltpu
from jax.sharding import PartitionSpec as P

F32, BF16 = jnp.float32, jnp.bfloat16
HB = 2048
LANES = 128
NPE = 125
EL = 32
GROUP = 8
NB, SB = 128, 16

LOWEST, CUT, TOP = -2.0, 4.0, 32.0
HALF = (TOP - CUT) / 2.0
CENTRE = (TOP + CUT) / 2.0
SIGMA = HALF / (LOWEST - CENTRE)
SIGMA_TWO = 1.0 / (2.0 / SIGMA - SIGMA)
A1 = SIGMA / HALF
A2 = 2.0 * SIGMA_TWO / HALF
A3 = SIGMA * SIGMA_TWO

VM = pl.BlockSpec(memory_space=pltpu.VMEM)
SM = pl.BlockSpec(memory_space=pltpu.SMEM)
ANY = pl.BlockSpec(memory_space=pl.ANY)
NODE_BLOCK = jax.ShapeDtypeStruct((HB, LANES), F32)
PARAMS = pltpu.CompilerParams(vmem_limit_bytes=56 << 20)
SHARE = 8


def split(value):
    high = value.astype(BF16)
    return high, (value - high.astype(F32)).astype(BF16)


def dot(a, b):
    return lax.dot_general(a, b, (((1,), (0,)), ((), ())), preferred_element_type=F32)


def dot_t(a, b):
    return lax.dot_general(a, b, (((1,), (1,)), ((), ())), preferred_element_type=F32)


def cost(microseconds):
    return pl.CostEstimate(flops=0, transcendentals=0, bytes_accessed=int(microseconds * 3.0e6))


def clear(sums):
    for ref in sums:
        ref[...] = jnp.zeros_like(ref)


def add_elements(conn, scale, matrix, values, picked, local, sums):
    high, low = split(matrix[...])
    left = jnp.concatenate(
        [
            jnp.concatenate([high, high], axis=1),
            jnp.concatenate([low, jnp.zeros_like(low)], axis=1),
        ],
        axis=0,
    )
    for ref in picked:
        ref[pl.ds(NPE, LANES - NPE), :] = jnp.zeros((LANES - NPE, LANES), F32)

    @pl.loop(0, EL // GROUP)
    def _(step):
        base = step * (GROUP * LANES)
        for i in range(NPE):
            for k in range(GROUP):
                node = conn[base + (k * LANES + i)]
                picked[k][pl.ds(i, 1), :] = values[pl.ds(node, 1), :]
        for k in range(0, GROUP, 2):
            pair = [split(picked[k + j][...]) for j in range(2)]
            right = jnp.concatenate(
                [
                    jnp.concatenate([pair[0][0], pair[1][0]], axis=1),
                    jnp.concatenate([pair[0][1], pair[1][1]], axis=1),
                ],
                axis=0,
            )
            product = dot(left, right)
            product = product[:LANES] + product[LANES:]
            for j in range(2):
                local[k + j][...] = (
                    product[:, j * LANES:(j + 1) * LANES] * scale[step * GROUP + (k + j)]
                )
        for i in range(NPE):
            for k in range(GROUP):
                node = conn[base + (k * LANES + i)]
                row = pl.ds(node, 1)
                sums[k][row, :] = sums[k][row, :] + local[k][pl.ds(i, 1), :]


def total(sums, start):
    parts = [ref[pl.ds(start, HB), :] for ref in sums]
    while len(parts) > 1:
        parts = [a + b for a, b in zip(parts[::2], parts[1::2])]
    return parts[0]


def fetch(pairs, sems):
    copies = [
        pltpu.make_async_copy(source, target, sems.at[i])
        for i, (source, target) in enumerate(pairs)
    ]
    for copy in copies:
        copy.start()
    return copies


LOW, HIGH = pl.ds(0, HB), pl.ds(HB, HB)


def kernel_a(conn, scale, matrix, u_l, u_u, low_ref, high_ref, sems, values, *scratch):
    picked, local, sums = scratch[:GROUP], scratch[GROUP:2 * GROUP], scratch[2 * GROUP:]
    copies = fetch([(u_l, values.at[LOW]), (u_u, values.at[HIGH])], sems)
    clear(sums)
    for copy in copies:
        copy.wait()
    add_elements(conn, scale, matrix, values, picked, local, sums)
    low_ref[...] = total(sums, 0)
    high_ref[...] = total(sums, HB)


def kernel_b(conn, scale, matrix, u_u, u_h, hi_a, m_u, w_u, x_ref, high_ref,
             sems, values, t0, t1, t2, *scratch):
    picked, local, sums = scratch[:GROUP], scratch[GROUP:2 * GROUP], scratch[2 * GROUP:]
    copies = fetch(
        [(u_u, values.at[LOW]), (u_h, values.at[HIGH]), (hi_a, t0), (m_u, t1), (w_u, t2)], sems
    )
    clear(sums)
    for copy in copies:
        copy.wait()
    add_elements(conn, scale, matrix, values, picked, local, sums)
    x_ref[...] = A1 * (t1[...] * (t0[...] + total(sums, 0)) + t2[...] * values[LOW, :])
    high_ref[...] = total(sums, HB)


def kernel_c(conn, scale, matrix, x_u, hi_b, lo_a, u_h, m_h, w_h, low_ref, high_ref,
             sems, values, t0, t1, t2, t3, t4, *scratch):
    picked, local, sums = scratch[:GROUP], scratch[GROUP:2 * GROUP], scratch[2 * GROUP:]
    copies = fetch(
        [(x_u, values.at[LOW]), (hi_b, t0), (lo_a, t1), (u_h, t2), (m_h, t3), (w_h, t4)], sems
    )
    clear(sums)
    for copy in copies:
        copy.wait()
    values[HIGH, :] = A1 * (t3[...] * (t0[...] + t1[...]) + t4[...] * t2[...])
    add_elements(conn, scale, matrix, values, picked, local, sums)
    low_ref[...] = total(sums, 0)
    high_ref[...] = total(sums, HB)


def kernel_d(conn, scale, matrix, x_u, lo_a, hi_b, u_l, m_l, w_l, low_ref, high_ref, x_ref,
             sems, values, t0, t1, t2, t3, t4, *scratch):
    picked, local, sums = scratch[:GROUP], scratch[GROUP:2 * GROUP], scratch[2 * GROUP:]
    copies = fetch(
        [(x_u, values.at[HIGH]), (lo_a, t0), (hi_b, t1), (u_l, t2), (m_l, t3), (w_l, t4)], sems
    )
    clear(sums)
    for copy in copies:
        copy.wait()
    x_l = A1 * (t3[...] * (t0[...] + t1[...]) + t4[...] * t2[...])
    values[LOW, :] = x_l
    x_ref[...] = x_l
    add_elements(conn, scale, matrix, values, picked, local, sums)
    low_ref[...] = total(sums, 0)
    high_ref[...] = total(sums, HB)


def element_call(kernel, outs, temporaries, *operands):
    count = len(operands) - 3
    return pl.pallas_call(
        kernel,
        out_shape=(NODE_BLOCK,) * outs,
        in_specs=[SM, SM, VM] + [ANY] * count,
        out_specs=(VM,) * outs,
        scratch_shapes=[pltpu.SemaphoreType.DMA((count,)), pltpu.VMEM((2 * HB, LANES), F32)]
        + [pltpu.VMEM((HB, LANES), F32)] * temporaries
        + [pltpu.VMEM((LANES, LANES), F32)] * (2 * GROUP)
        + [pltpu.VMEM((2 * HB, LANES), F32)] * GROUP,
        compiler_params=PARAMS,
        cost_estimate=cost(13),
    )(*operands)


def spread_kernel(mass, well, *outs):
    count = HB // LANES
    for chunk in range(mass.shape[0]):
        rows = pl.ds(chunk % count * LANES, LANES)
        one = jnp.broadcast_to(mass[pl.ds(chunk, 1), :], (LANES, LANES))
        outs[chunk // count * 2][rows, :] = (one * one).T
        two = jnp.broadcast_to(well[pl.ds(chunk, 1), :] - CENTRE, (LANES, LANES))
        outs[chunk // count * 2 + 1][rows, :] = two.T


def spread(mass, well):
    outs = 2 * (mass.shape[0] * LANES // HB)
    return pl.pallas_call(
        spread_kernel,
        out_shape=(NODE_BLOCK,) * outs,
        in_specs=[VM, VM],
        out_specs=(VM,) * outs,
        compiler_params=PARAMS,
        cost_estimate=cost(outs),
    )(mass, well)


def enter_kernel(core, block, other, mass, low_ref, high_ref, mine, sem):
    owned = 2 * HB
    start = pl.multiple_of(core[0] * owned, owned)
    copy = pltpu.make_async_copy(block.at[:, pl.ds(start, owned)], mine, sem)
    copy.start()
    copy.wait()
    first = core[0] == 0
    for chunk in range(owned // LANES):
        columns = pl.ds(chunk * LANES, LANES)
        a, b = mine[:, columns], other[:, columns]
        stacked = jnp.concatenate([jnp.where(first, a, b), jnp.where(first, b, a)], axis=0)
        target = low_ref if chunk < HB // LANES else high_ref
        rows = pl.ds(chunk % (HB // LANES) * LANES, LANES)
        target[rows, :] = (stacked * mass[pl.ds(chunk, 1), :]).T


def enter(core, block, other, mass):
    return pl.pallas_call(
        enter_kernel,
        out_shape=(NODE_BLOCK, NODE_BLOCK),
        in_specs=[SM, ANY, VM, VM],
        out_specs=(VM, VM),
        scratch_shapes=[pltpu.VMEM((block.shape[0], 2 * HB), F32), pltpu.SemaphoreType.DMA],
        compiler_params=PARAMS,
        cost_estimate=cost(4),
    )(core, block, other, mass)


FINISH = 512


def finish_kernel(row, lo_d, hi_c, hi_d, lo_c, u_l, u_u, x_l, x_u, m_l, m_u, w_l, w_u, mass,
                  out_ref, away_ref):
    step = pl.program_id(0)
    count = FINISH // LANES
    for chunk in range(count):
        rows = pl.ds(chunk * LANES, LANES)
        turned = []
        for half, (a, b, u, x, m, w) in enumerate(
            ((lo_d, hi_c, u_l, x_l, m_l, w_l), (hi_d, lo_c, u_u, x_u, m_u, w_u))
        ):
            value = A2 * (m[rows, :] * (a[rows, :] + b[rows, :]) + w[rows, :] * x[rows, :])
            value = (value - A3 * u[rows, :]).T
            at = half * (HB // LANES) + step * count + chunk
            value = value / mass[pl.ds(at, 1), :]
            order = [
                value[kk * 4 * SB + c * SB:kk * 4 * SB + (c + 1) * SB, :]
                for c in range(4) for kk in range(2)
            ]
            value = jnp.concatenate(order, axis=0)
            turned.append(value)
            for c in range(4):
                out_ref[half, chunk * 4 + c, pl.ds(0, 2 * SB), :] = value[
                    c * 2 * SB:(c + 1) * 2 * SB, :
                ]
        away_ref[chunk] = jnp.where(row[0] == 0, turned[1], turned[0])


def finish(row, *operands):
    part = pl.BlockSpec((FINISH, LANES), lambda i: (i, 0))
    count = FINISH // LANES
    targets = HB // LANES * 4
    return pl.pallas_call(
        finish_kernel,
        out_shape=(
            jax.ShapeDtypeStruct((2, targets, 2 * SB + SHARE, LANES), F32),
            jax.ShapeDtypeStruct((HB // LANES, LANES, LANES), F32),
        ),
        grid=(HB // FINISH,),
        in_specs=[SM] + [part] * (len(operands) - 1) + [VM],
        out_specs=(
            pl.BlockSpec((2, count * 4, 2 * SB + SHARE, LANES), lambda i: (0, i, 0, 0)),
            pl.BlockSpec((count, LANES, LANES), lambda i: (i, 0, 0)),
        ),
        compiler_params=PARAMS,
        cost_estimate=cost(5),
    )(row, *operands)


def overlap_kernel(weight, row, tiles, received, out_ref, mine, main, cross, panel, shares, sems):
    copy = pltpu.make_async_copy(tiles.at[row[0], :, pl.ds(0, 2 * SB), :], mine, sems.at[0])
    copy.start()
    main[...] = jnp.zeros_like(main)
    cross[...] = jnp.zeros_like(cross)
    first = row[0] == 0
    copy.wait()

    @pl.loop(0, received.shape[0] // 2)
    def _(step):
        blocks = []
        for c in range(4):
            rows = pl.ds(c * 2 * SB, 2 * SB)
            a = jnp.concatenate([mine[8 * step + c], mine[8 * step + (4 + c)]], axis=1)
            b = jnp.concatenate(
                [received[2 * step, rows, :], received[2 * step + 1, rows, :]], axis=1
            )
            blocks += [jnp.where(first, a, b), jnp.where(first, b, a)]
        high, low = split(jnp.concatenate(blocks, axis=0))
        main[...] += dot_t(high, high)
        cross[...] += dot_t(high, low)

    panel[...] = (main[...] + (cross[...] + cross[...].T)) * weight
    for n in range(HB // LANES):
        for c in range(4):
            shares[n * 4 + c] = panel[
                pl.ds(c * 4 * SB + n // 2 * SHARE, SHARE), pl.ds(n % 2 * LANES, LANES)
            ]
    copies = [
        pltpu.make_async_copy(shares, out_ref.at[h, :, pl.ds(2 * SB, SHARE), :], sems.at[h])
        for h in range(2)
    ]
    for copy in copies:
        copy.start()
    for copy in copies:
        copy.wait()


def overlap(weight, row, tiles, received):
    states = 2 * LANES
    targets = tiles.shape[1]
    return pl.pallas_call(
        functools.partial(overlap_kernel, weight),
        out_shape=jax.ShapeDtypeStruct(tiles.shape, F32),
        in_specs=[SM, ANY, VM],
        out_specs=ANY,
        input_output_aliases={1: 0},
        scratch_shapes=[pltpu.VMEM((targets, 2 * SB, LANES), F32)]
        + [pltpu.VMEM((states, states), F32)] * 3
        + [pltpu.VMEM((targets, SHARE, LANES), F32), pltpu.SemaphoreType.DMA((2,))],
        compiler_params=PARAMS,
        cost_estimate=cost(4),
    )(row, tiles, received)


def place_kernel(moved, out_ref):
    for p in range(moved.shape[0] // 4):
        for y in range(2):
            for core in range(2):
                out_ref[pl.ds(y * 2 * SB, 2 * SB), pl.ds((2 * p + core) * NB, NB)] = moved[
                    p * 4 + y * 2 + core, pl.ds(0, 2 * SB), :
                ]


def place(moved):
    steps, sources = 4, moved.shape[0]
    return pl.pallas_call(
        place_kernel,
        out_shape=jax.ShapeDtypeStruct((4 * SB, sources // 2 * NB), F32),
        grid=(steps,),
        in_specs=[pl.BlockSpec((sources // steps,) + moved.shape[1:], lambda i: (i, 0, 0))],
        out_specs=pl.BlockSpec((4 * SB, sources // 2 * NB // steps), lambda i: (0, i)),
        compiler_params=PARAMS,
        cost_estimate=cost(2),
    )(moved)


def shards(block, inv_sqrt_mass, potential, elem_scale, connectivity, elem_matrix):
    both = ("nodes", "grid")
    parts = lax.axis_size("nodes")
    grid = lax.axis_index("grid")
    row, core = grid // 2, grid % 2
    owned = 2 * HB

    def along(step):
        pairs = []
        for y in range(2):
            for source in range(2 * parts):
                target = source + step
                if 0 <= target < 2 * parts:
                    pairs.append((
                        source // 2 * 4 + y * 2 + source % 2,
                        target // 2 * 4 + y * 2 + target % 2,
                    ))
        return lambda value: lax.ppermute(value, both, pairs)

    to_previous, to_next = along(-1), along(1)

    other = lax.dynamic_slice(block, (0, (1 - core) * owned), (block.shape[0], owned))
    other = lax.ppermute(other, "grid", [(0, 1), (1, 0), (2, 3), (3, 2)])
    fields = jnp.stack([inv_sqrt_mass, potential]).reshape(2, -1, LANES)
    count = HB // LANES
    rim = lax.ppermute(fields[:, :count], "nodes", [(n, n - 1) for n in range(1, parts)])
    own = lax.dynamic_slice(fields, (0, core * 2 * count, 0), (2, 2 * count, LANES))
    last = jnp.where(core == 0, fields[:, 2 * count:3 * count], rim)
    m_l, w_l, m_u, w_u = spread(own[0], own[1])

    conn = lax.dynamic_slice(connectivity, (core * 2 * EL, 0), (2 * EL, NPE)) - core * owned
    conn = jnp.pad(conn, ((0, 0), (0, LANES - NPE)))
    c_l, c_u = conn[:EL].reshape(-1), (conn[EL:] - HB).reshape(-1)
    scale = lax.dynamic_slice(elem_scale, (core * 2 * EL,), (2 * EL,))
    s_l, s_u = scale[:EL], scale[EL:]
    matrix = jnp.pad(elem_matrix, ((0, LANES - NPE), (0, LANES - NPE)))

    u_l, u_u = enter(core[None], block, other, own[0])
    u_h = to_previous(u_l)
    lo_a, hi_a = element_call(kernel_a, 2, 0, c_l, s_l, matrix, u_l, u_u)
    lo_a_next = to_previous(lo_a)
    m_h, w_h = spread(last[0], last[1])
    x_u, hi_b = element_call(kernel_b, 2, 3, c_u, s_u, matrix, u_u, u_h, hi_a, m_u, w_u)
    hi_b_previous = to_next(hi_b)
    lo_c, hi_c = element_call(
        kernel_c, 2, 5, c_u, s_u, matrix, x_u, hi_b, lo_a_next, u_h, m_h, w_h
    )
    hi_c_previous = to_next(hi_c)
    lo_d, hi_d, x_l = element_call(
        kernel_d, 3, 5, c_l, s_l, matrix, x_u, lo_a, hi_b_previous, u_l, m_l, w_l
    )
    tiles, away = finish(
        row[None], lo_d, hi_c_previous, hi_d, lo_c, u_l, u_u, x_l, x_u, m_l, m_u, w_l, w_u, own[0]
    )
    received = lax.ppermute(away, "grid", [(0, 2), (1, 3), (2, 0), (3, 1)])

    tiles = overlap(1.0 / (parts * 4 * HB), row[None], tiles, received)
    moved = lax.all_to_all(
        tiles.reshape(4 * parts, 2 * SB + SHARE, NB), both, split_axis=0, concat_axis=0, tiled=True
    )
    share = jnp.sum(moved[:, 2 * SB:, :], axis=0)
    shares = lax.all_to_all(
        jnp.broadcast_to(share[None], (parts, SHARE, LANES)),
        "nodes", split_axis=0, concat_axis=0, tiled=True,
    )
    rows = shares[:count].reshape(count // 2, 2, SHARE, LANES).transpose(0, 2, 1, 3)
    intersection = rows.reshape(4 * SB, 2 * LANES).T
    return (place(moved), intersection)


def solution(mesh):
    placed = (P("grid", "nodes"), P("nodes"), P("nodes"), P("nodes"), P("nodes", None), P())
    return jax.shard_map(
        shards,
        mesh=mesh,
        in_specs=placed,
        out_specs=(P("grid", "nodes"), P(None, "grid")),
        check_vma=False,
    )
```

```python
import functools

import jax
import jax.numpy as jnp
from jax import lax
from jax.experimental import pallas as pl
from jax.experimental.pallas import tpu as pltpu
from jax.sharding import PartitionSpec as P

F32, BF16 = jnp.float32, jnp.bfloat16
HB = 2048
LANES = 128
NPE = 125
EL = 32
STRIDE = 64
GROUP = 8
NB, SB = 128, 16

LOWEST, CUT, TOP = -2.0, 4.0, 32.0
HALF = (TOP - CUT) / 2.0
CENTRE = (TOP + CUT) / 2.0
SIGMA = HALF / (LOWEST - CENTRE)
SIGMA_TWO = 1.0 / (2.0 / SIGMA - SIGMA)
A1 = SIGMA / HALF
A2 = 2.0 * SIGMA_TWO / HALF
A3 = SIGMA * SIGMA_TWO

VM = pl.BlockSpec(memory_space=pltpu.VMEM)
SM = pl.BlockSpec(memory_space=pltpu.SMEM)
ANY = pl.BlockSpec(memory_space=pl.ANY)
NODE_BLOCK = jax.ShapeDtypeStruct((HB, LANES), F32)
PARAMS = pltpu.CompilerParams(vmem_limit_bytes=56 << 20)
SHARE = 8


def split(value):
    high = value.astype(BF16)
    return high, (value - high.astype(F32)).astype(BF16)


def dot(a, b):
    return lax.dot_general(a, b, (((1,), (0,)), ((), ())), preferred_element_type=F32)


def dot_t(a, b):
    return lax.dot_general(a, b, (((1,), (1,)), ((), ())), preferred_element_type=F32)


def cost(microseconds):
    return pl.CostEstimate(flops=0, transcendentals=0, bytes_accessed=int(microseconds * 3.0e6))


RUN = EL // GROUP
REACH = 2304
PIECE = 256


def clear(sums):
    for k, ref in enumerate(sums):
        start = k * RUN * STRIDE
        size = min(REACH, 2 * HB - start)
        ref[pl.ds(start, size), :] = jnp.zeros((size, LANES), F32)


def add_elements(conn, scale, matrix, values, picked, local, sums):
    high, low = split(matrix[...])
    left = jnp.concatenate(
        [
            jnp.concatenate([high, high], axis=1),
            jnp.concatenate([low, jnp.zeros_like(low)], axis=1),
        ],
        axis=0,
    )
    for ref in picked:
        ref[pl.ds(NPE, LANES - NPE), :] = jnp.zeros((LANES - NPE, LANES), F32)

    @pl.loop(0, RUN)
    def _(step):
        base = step * LANES
        for i in range(NPE):
            for k in range(GROUP):
                node = conn[base + (k * RUN * LANES + i)]
                picked[k][pl.ds(i, 1), :] = values[pl.ds(node, 1), :]
        for k in range(0, GROUP, 2):
            pair = [split(picked[k + j][...]) for j in range(2)]
            right = jnp.concatenate(
                [
                    jnp.concatenate([pair[0][0], pair[1][0]], axis=1),
                    jnp.concatenate([pair[0][1], pair[1][1]], axis=1),
                ],
                axis=0,
            )
            product = dot(left, right)
            product = product[:LANES] + product[LANES:]
            for j in range(2):
                local[k + j][...] = (
                    product[:, j * LANES:(j + 1) * LANES] * scale[step + (k + j) * RUN]
                )
        for i in range(NPE):
            for k in range(GROUP):
                node = conn[base + (k * RUN * LANES + i)]
                row = pl.ds(node, 1)
                sums[k][row, :] = sums[k][row, :] + local[k][pl.ds(i, 1), :]


def total(sums, start):
    pieces = []
    for row in range(start, start + HB, PIECE):
        parts = [
            ref[pl.ds(row, PIECE), :]
            for k, ref in enumerate(sums)
            if 0 <= row - k * RUN * STRIDE < REACH
        ]
        while len(parts) > 1:
            parts = [a + b for a, b in zip(parts[::2], parts[1::2])] + (
                [parts[-1]] if len(parts) % 2 else []
            )
        pieces.append(parts[0])
    return jnp.concatenate(pieces, axis=0)


def fetch(pairs, sems):
    copies = [
        pltpu.make_async_copy(source, target, sems.at[i])
        for i, (source, target) in enumerate(pairs)
    ]
    for copy in copies:
        copy.start()
    return copies


LOW, HIGH = pl.ds(0, HB), pl.ds(HB, HB)


def kernel_a(conn, scale, matrix, u_l, u_u, low_ref, high_ref, sems, values, *scratch):
    picked, local, sums = scratch[:GROUP], scratch[GROUP:2 * GROUP], scratch[2 * GROUP:]
    copies = fetch([(u_l, values.at[LOW]), (u_u, values.at[HIGH])], sems)
    clear(sums)
    for copy in copies:
        copy.wait()
    add_elements(conn, scale, matrix, values, picked, local, sums)
    low_ref[...] = total(sums, 0)
    high_ref[...] = total(sums, HB)


def kernel_b(conn, scale, matrix, u_u, u_h, hi_a, m_u, w_u, x_ref, high_ref,
             sems, values, t0, t1, t2, *scratch):
    picked, local, sums = scratch[:GROUP], scratch[GROUP:2 * GROUP], scratch[2 * GROUP:]
    copies = fetch(
        [(u_u, values.at[LOW]), (u_h, values.at[HIGH]), (hi_a, t0), (m_u, t1), (w_u, t2)], sems
    )
    clear(sums)
    for copy in copies:
        copy.wait()
    add_elements(conn, scale, matrix, values, picked, local, sums)
    x_ref[...] = A1 * (t1[...] * (t0[...] + total(sums, 0)) + t2[...] * values[LOW, :])
    high_ref[...] = total(sums, HB)


def kernel_c(conn, scale, matrix, x_u, hi_b, lo_a, u_h, m_h, w_h, low_ref, high_ref,
             sems, values, t0, t1, t2, t3, t4, *scratch):
    picked, local, sums = scratch[:GROUP], scratch[GROUP:2 * GROUP], scratch[2 * GROUP:]
    copies = fetch(
        [(x_u, values.at[LOW]), (hi_b, t0), (lo_a, t1), (u_h, t2), (m_h, t3), (w_h, t4)], sems
    )
    clear(sums)
    for copy in copies:
        copy.wait()
    values[HIGH, :] = A1 * (t3[...] * (t0[...] + t1[...]) + t4[...] * t2[...])
    add_elements(conn, scale, matrix, values, picked, local, sums)
    low_ref[...] = total(sums, 0)
    high_ref[...] = total(sums, HB)


def kernel_d(conn, scale, matrix, x_u, lo_a, hi_b, u_l, m_l, w_l, lo_c, u_u, m_u, w_u,
             low_ref, high_ref, sems, values, t0, t1, t2, t3, t4, t5, t6, t7, t8, *scratch):
    picked, local, sums = scratch[:GROUP], scratch[GROUP:2 * GROUP], scratch[2 * GROUP:]
    copies = fetch(
        [(x_u, values.at[HIGH]), (lo_a, t0), (hi_b, t1), (u_l, t2), (m_l, t3), (w_l, t4),
         (lo_c, t5), (u_u, t6), (m_u, t7), (w_u, t8)],
        sems,
    )
    clear(sums)
    for copy in copies[:6]:
        copy.wait()
    values[LOW, :] = A1 * (t3[...] * (t0[...] + t1[...]) + t4[...] * t2[...])
    add_elements(conn, scale, matrix, values, picked, local, sums)
    for copy in copies[6:]:
        copy.wait()
    low_ref[...] = A2 * (t3[...] * total(sums, 0) + t4[...] * values[LOW, :]) - A3 * t2[...]
    high_ref[...] = (
        A2 * (t7[...] * (t5[...] + total(sums, HB)) + t8[...] * values[HIGH, :]) - A3 * t6[...]
    )


def element_call(kernel, outs, temporaries, *operands):
    count = len(operands) - 3
    return pl.pallas_call(
        kernel,
        out_shape=(NODE_BLOCK,) * outs,
        in_specs=[SM, SM, VM] + [ANY] * count,
        out_specs=(VM,) * outs,
        scratch_shapes=[pltpu.SemaphoreType.DMA((count,)), pltpu.VMEM((2 * HB, LANES), F32)]
        + [pltpu.VMEM((HB, LANES), F32)] * temporaries
        + [pltpu.VMEM((LANES, LANES), F32)] * (2 * GROUP)
        + [pltpu.VMEM((2 * HB, LANES), F32)] * GROUP,
        compiler_params=PARAMS,
        cost_estimate=cost(13),
    )(*operands)


def spread_kernel(mass, well, *outs):
    count = HB // LANES
    for chunk in range(mass.shape[0]):
        rows = pl.ds(chunk % count * LANES, LANES)
        one = jnp.broadcast_to(mass[pl.ds(chunk, 1), :], (LANES, LANES))
        outs[chunk // count * 2][rows, :] = (one * one).T
        two = jnp.broadcast_to(well[pl.ds(chunk, 1), :] - CENTRE, (LANES, LANES))
        outs[chunk // count * 2 + 1][rows, :] = two.T


def spread(mass, well):
    outs = 2 * (mass.shape[0] * LANES // HB)
    return pl.pallas_call(
        spread_kernel,
        out_shape=(NODE_BLOCK,) * outs,
        in_specs=[VM, VM],
        out_specs=(VM,) * outs,
        compiler_params=PARAMS,
        cost_estimate=cost(outs),
    )(mass, well)


def enter_kernel(core, block, other, mass, low_ref, high_ref, mine, sem):
    owned = 2 * HB
    start = pl.multiple_of(core[0] * owned, owned)
    copy = pltpu.make_async_copy(block.at[:, pl.ds(start, owned)], mine, sem)
    copy.start()
    copy.wait()
    first = core[0] == 0
    for chunk in range(owned // LANES):
        columns = pl.ds(chunk * LANES, LANES)
        a, b = mine[:, columns], other[:, columns]
        stacked = jnp.concatenate([jnp.where(first, a, b), jnp.where(first, b, a)], axis=0)
        target = low_ref if chunk < HB // LANES else high_ref
        rows = pl.ds(chunk % (HB // LANES) * LANES, LANES)
        target[rows, :] = (stacked * mass[pl.ds(chunk, 1), :]).T


def enter(core, block, other, mass):
    return pl.pallas_call(
        enter_kernel,
        out_shape=(NODE_BLOCK, NODE_BLOCK),
        in_specs=[SM, ANY, VM, VM],
        out_specs=(VM, VM),
        scratch_shapes=[pltpu.VMEM((block.shape[0], 2 * HB), F32), pltpu.SemaphoreType.DMA],
        compiler_params=PARAMS,
        cost_estimate=cost(4),
    )(core, block, other, mass)


FINISH = 512


def finish_kernel(row, f_l, hi_c, m_l, f_u, mass, out_ref, away_ref):
    step = pl.program_id(0)
    count = FINISH // LANES
    for chunk in range(count):
        rows = pl.ds(chunk * LANES, LANES)
        turned = []
        for half in range(2):
            value = f_l[rows, :] + A2 * (m_l[rows, :] * hi_c[rows, :]) if half == 0 else f_u[rows, :]
            at = half * (HB // LANES) + step * count + chunk
            value = value.T / mass[pl.ds(at, 1), :]
            order = [
                value[kk * 4 * SB + c * SB:kk * 4 * SB + (c + 1) * SB, :]
                for c in range(4) for kk in range(2)
            ]
            value = jnp.concatenate(order, axis=0)
            turned.append(value)
            out_ref[half, chunk] = value
        away_ref[chunk] = jnp.where(row[0] == 0, turned[1], turned[0])


def finish(row, *operands):
    part = pl.BlockSpec((FINISH, LANES), lambda i: (i, 0))
    count = FINISH // LANES
    return pl.pallas_call(
        finish_kernel,
        out_shape=(
            jax.ShapeDtypeStruct((2, HB // LANES, LANES, LANES), F32),
            jax.ShapeDtypeStruct((HB // LANES, LANES, LANES), F32),
        ),
        grid=(HB // FINISH,),
        in_specs=[SM] + [part] * (len(operands) - 1) + [VM],
        out_specs=(
            pl.BlockSpec((2, count, LANES, LANES), lambda i: (0, i, 0, 0)),
            pl.BlockSpec((count, LANES, LANES), lambda i: (i, 0, 0)),
        ),
        compiler_params=PARAMS,
        cost_estimate=cost(3),
    )(row, *operands)


def overlap_kernel(weight, row, tiles, received, shares, mine, main, cross, panel, sem):
    copy = pltpu.make_async_copy(tiles.at[row[0]], mine, sem)
    copy.start()
    main[...] = jnp.zeros_like(main)
    cross[...] = jnp.zeros_like(cross)
    first = row[0] == 0
    copy.wait()

    @pl.loop(0, received.shape[0] // 2)
    def _(step):
        blocks = []
        for c in range(4):
            rows = pl.ds(c * 2 * SB, 2 * SB)
            a = jnp.concatenate([mine[2 * step, rows, :], mine[2 * step + 1, rows, :]], axis=1)
            b = jnp.concatenate(
                [received[2 * step, rows, :], received[2 * step + 1, rows, :]], axis=1
            )
            blocks += [jnp.where(first, a, b), jnp.where(first, b, a)]
        high, low = split(jnp.concatenate(blocks, axis=0))
        main[...] += dot_t(high, high)
        cross[...] += dot_t(high, low)

    panel[...] = (main[...] + (cross[...] + cross[...].T)) * weight
    count = HB // LANES
    for n in range(2 * count):
        for c in range(4):
            shares[n * 4 + c] = panel[
                pl.ds(c * 4 * SB + n % count // 2 * SHARE, SHARE), pl.ds(n % 2 * LANES, LANES)
            ]


def overlap(weight, row, tiles, received):
    states = 2 * LANES
    return pl.pallas_call(
        functools.partial(overlap_kernel, weight),
        out_shape=jax.ShapeDtypeStruct((8 * tiles.shape[1], SHARE, LANES), F32),
        in_specs=[SM, ANY, VM],
        out_specs=VM,
        scratch_shapes=[pltpu.VMEM(tiles.shape[1:], F32)]
        + [pltpu.VMEM((states, states), F32)] * 3
        + [pltpu.SemaphoreType.DMA],
        compiler_params=PARAMS,
        cost_estimate=cost(5),
    )(row, tiles, received)


def place_kernel(moved, *refs):
    out_ref = refs[-1]
    for p in range(moved.shape[0] // 4):
        for y in range(2):
            for core in range(2):
                out_ref[pl.ds(y * 2 * SB, 2 * SB), pl.ds((2 * p + core) * NB, NB)] = moved[
                    p * 4 + y * 2 + core
                ]


def place(half, moved, *placed):
    steps, sources = 2, moved.shape[0]
    width = sources // 2 * NB // (2 * steps)
    return pl.pallas_call(
        place_kernel,
        out_shape=jax.ShapeDtypeStruct((4 * SB, sources // 2 * NB), F32),
        grid=(steps,),
        in_specs=[
            pl.BlockSpec(
                (sources // (2 * steps),) + moved.shape[1:], lambda i: (half * steps + i, 0, 0)
            )
        ] + [ANY] * len(placed),
        out_specs=pl.BlockSpec((4 * SB, width), lambda i: (0, half * steps + i)),
        input_output_aliases={1: 0} if placed else {},
        compiler_params=PARAMS,
        cost_estimate=cost(3),
    )(moved, *placed)


def shards(block, inv_sqrt_mass, potential, elem_scale, connectivity, elem_matrix):
    both = ("nodes", "grid")
    parts = lax.axis_size("nodes")
    grid = lax.axis_index("grid")
    row, core = grid // 2, grid % 2
    owned = 2 * HB

    def along(step):
        pairs = []
        for y in range(2):
            for source in range(2 * parts):
                target = source + step
                if 0 <= target < 2 * parts:
                    pairs.append((
                        source // 2 * 4 + y * 2 + source % 2,
                        target // 2 * 4 + y * 2 + target % 2,
                    ))
        return lambda value: lax.ppermute(value, both, pairs)

    to_previous, to_next = along(-1), along(1)

    other = lax.dynamic_slice(block, (0, (1 - core) * owned), (block.shape[0], owned))
    other = lax.ppermute(other, "grid", [(0, 1), (1, 0), (2, 3), (3, 2)])
    fields = jnp.stack([inv_sqrt_mass, potential]).reshape(2, -1, LANES)
    count = HB // LANES
    rim = lax.ppermute(fields[:, :count], "nodes", [(n, n - 1) for n in range(1, parts)])
    own = lax.dynamic_slice(fields, (0, core * 2 * count, 0), (2, 2 * count, LANES))
    other, rim_done = lax.optimization_barrier((other, rim))
    m_l, w_l, m_u, w_u = spread(own[0], own[1])
    last = jnp.where(core == 0, fields[:, 2 * count:3 * count], rim_done)

    conn = lax.dynamic_slice(connectivity, (core * 2 * EL, 0), (2 * EL, NPE)) - core * owned
    conn = jnp.pad(conn, ((0, 0), (0, LANES - NPE)))
    c_l, c_u = conn[:EL].reshape(-1), (conn[EL:] - HB).reshape(-1)
    scale = lax.dynamic_slice(elem_scale, (core * 2 * EL,), (2 * EL,))
    s_l, s_u = scale[:EL], scale[EL:]
    matrix = jnp.pad(elem_matrix, ((0, LANES - NPE), (0, LANES - NPE)))

    u_l, u_u = enter(core[None], block, other, own[0])
    u_h = to_previous(u_l)
    lo_a, hi_a = element_call(kernel_a, 2, 0, c_l, s_l, matrix, u_l, u_u)
    lo_a_next = to_previous(lo_a)
    m_h, w_h = spread(last[0], last[1])
    x_u, hi_b = element_call(kernel_b, 2, 3, c_u, s_u, matrix, u_u, u_h, hi_a, m_u, w_u)
    hi_b_previous = to_next(hi_b)
    lo_c, hi_c = element_call(
        kernel_c, 2, 5, c_u, s_u, matrix, x_u, hi_b, lo_a_next, u_h, m_h, w_h
    )
    hi_c_previous = to_next(hi_c)
    f_l, f_u = element_call(
        kernel_d, 2, 9, c_l, s_l, matrix,
        x_u, lo_a, hi_b_previous, u_l, m_l, w_l, lo_c, u_u, m_u, w_u,
    )
    tiles, away = finish(row[None], f_l, hi_c_previous, m_l, f_u, own[0])
    received = lax.ppermute(away, "grid", [(0, 2), (1, 3), (2, 0), (3, 1)])
    tiles, received = lax.optimization_barrier((tiles, received))

    moved = lax.all_to_all(
        tiles.reshape(4 * parts, 2 * SB, NB), both, split_axis=0, concat_axis=0, tiled=True
    )
    shares = overlap(1.0 / (parts * 4 * HB), row[None], tiles, received)
    moved, shares = lax.optimization_barrier((moved, shares))
    shares = lax.all_to_all(shares, both, split_axis=0, concat_axis=0, tiled=True)
    cyclic = place(0, moved)
    share = jnp.sum(shares, axis=0)
    share, moved, cyclic = lax.optimization_barrier((share, moved, cyclic))
    shares = lax.all_to_all(
        jnp.broadcast_to(share[None], (parts, SHARE, LANES)),
        "nodes", split_axis=0, concat_axis=0, tiled=True,
    )
    cyclic = place(1, moved, cyclic)
    rows = shares[:count].reshape(count // 2, 2, SHARE, LANES).transpose(0, 2, 1, 3)
    intersection = rows.reshape(4 * SB, 2 * LANES).T
    return (cyclic, intersection)


def solution(mesh):
    placed = (P("grid", "nodes"), P("nodes"), P("nodes"), P("nodes"), P("nodes", None), P())
    return jax.shard_map(
        shards,
        mesh=mesh,
        in_specs=placed,
        out_specs=(P("grid", "nodes"), P(None, "grid")),
        check_vma=False,
    )
```

```python
import functools

import jax
import jax.numpy as jnp
from jax import lax
from jax.experimental import pallas as pl
from jax.experimental.pallas import tpu as pltpu
from jax.sharding import PartitionSpec as P

F32, BF16 = jnp.float32, jnp.bfloat16
HB = 2048
LANES = 128
NPE = 125
EL = 32
STRIDE = 64
GROUP = 8
NB, SB = 128, 16

LOWEST, CUT, TOP = -2.0, 4.0, 32.0
HALF = (TOP - CUT) / 2.0
CENTRE = (TOP + CUT) / 2.0
SIGMA = HALF / (LOWEST - CENTRE)
SIGMA_TWO = 1.0 / (2.0 / SIGMA - SIGMA)
A1 = SIGMA / HALF
A2 = 2.0 * SIGMA_TWO / HALF
A3 = SIGMA * SIGMA_TWO

VM = pl.BlockSpec(memory_space=pltpu.VMEM)
SM = pl.BlockSpec(memory_space=pltpu.SMEM)
ANY = pl.BlockSpec(memory_space=pl.ANY)
NODE_BLOCK = jax.ShapeDtypeStruct((HB, LANES), F32)
PARAMS = pltpu.CompilerParams(vmem_limit_bytes=40 << 20)
SHARE = 4


def split(value):
    high = value.astype(BF16)
    return high, (value - high.astype(F32)).astype(BF16)


def dot(a, b):
    return lax.dot_general(a, b, (((1,), (0,)), ((), ())), preferred_element_type=F32)


def dot_t(a, b):
    return lax.dot_general(a, b, (((1,), (1,)), ((), ())), preferred_element_type=F32)


def cost(microseconds):
    return pl.CostEstimate(flops=0, transcendentals=0, bytes_accessed=int(microseconds * 3.0e6))


RUN = EL // GROUP
REACH = 2304
PIECE = 256


def clear(sums):
    for k, ref in enumerate(sums):
        start = k * RUN * STRIDE
        size = min(REACH, 2 * HB - start)
        ref[pl.ds(start, size), :] = jnp.zeros((size, LANES), F32)


def add_elements(conn, scale, matrix, values, picked, local, sums):
    high, low = split(matrix[...])
    left = jnp.concatenate(
        [
            jnp.concatenate([high, high], axis=1),
            jnp.concatenate([low, jnp.zeros_like(low)], axis=1),
        ],
        axis=0,
    )
    for ref in picked:
        ref[pl.ds(NPE, LANES - NPE), :] = jnp.zeros((LANES - NPE, LANES), F32)

    @pl.loop(0, RUN)
    def _(step):
        base = step * LANES
        for i in range(NPE):
            for k in range(GROUP):
                node = conn[base + (k * RUN * LANES + i)]
                picked[k][pl.ds(i, 1), :] = values[pl.ds(node, 1), :]
        for k in range(0, GROUP, 2):
            pair = [split(picked[k + j][...]) for j in range(2)]
            right = jnp.concatenate(
                [
                    jnp.concatenate([pair[0][0], pair[1][0]], axis=1),
                    jnp.concatenate([pair[0][1], pair[1][1]], axis=1),
                ],
                axis=0,
            )
            product = dot(left, right)
            product = product[:LANES] + product[LANES:]
            for j in range(2):
                local[k + j][...] = (
                    product[:, j * LANES:(j + 1) * LANES] * scale[step + (k + j) * RUN]
                )
        for i in range(NPE):
            for k in range(GROUP):
                node = conn[base + (k * RUN * LANES + i)]
                row = pl.ds(node, 1)
                sums[k][row, :] = sums[k][row, :] + local[k][pl.ds(i, 1), :]


def total(sums, start):
    pieces = []
    for row in range(start, start + HB, PIECE):
        parts = [
            ref[pl.ds(row, PIECE), :]
            for k, ref in enumerate(sums)
            if 0 <= row - k * RUN * STRIDE < REACH
        ]
        while len(parts) > 1:
            parts = [a + b for a, b in zip(parts[::2], parts[1::2])] + (
                [parts[-1]] if len(parts) % 2 else []
            )
        pieces.append(parts[0])
    return jnp.concatenate(pieces, axis=0)


def fetch(pairs, sems):
    copies = [
        pltpu.make_async_copy(source, target, sems.at[i])
        for i, (source, target) in enumerate(pairs)
    ]
    for copy in copies:
        copy.start()
    return copies


LOW, HIGH = pl.ds(0, HB), pl.ds(HB, HB)


def kernel_a(conn, scale, matrix, u_l, u_u, low_ref, high_ref, sems, values, *scratch):
    picked, local, sums = scratch[:GROUP], scratch[GROUP:2 * GROUP], scratch[2 * GROUP:]
    copies = fetch([(u_l, values.at[LOW]), (u_u, values.at[HIGH])], sems)
    clear(sums)
    for copy in copies:
        copy.wait()
    add_elements(conn, scale, matrix, values, picked, local, sums)
    low_ref[...] = total(sums, 0)
    high_ref[...] = total(sums, HB)


def kernel_b(conn, scale, matrix, u_u, u_h, hi_a, m_u, w_u, x_ref, high_ref,
             sems, values, t0, t1, t2, *scratch):
    picked, local, sums = scratch[:GROUP], scratch[GROUP:2 * GROUP], scratch[2 * GROUP:]
    copies = fetch(
        [(u_u, values.at[LOW]), (u_h, values.at[HIGH]), (hi_a, t0), (m_u, t1), (w_u, t2)], sems
    )
    clear(sums)
    for copy in copies:
        copy.wait()
    add_elements(conn, scale, matrix, values, picked, local, sums)
    x_ref[...] = A1 * (t1[...] * (t0[...] + total(sums, 0)) + t2[...] * values[LOW, :])
    high_ref[...] = total(sums, HB)


def kernel_c(conn, scale, matrix, x_u, hi_b, lo_a, u_h, m_h, w_h, low_ref, high_ref,
             sems, values, t0, t1, t2, t3, t4, *scratch):
    picked, local, sums = scratch[:GROUP], scratch[GROUP:2 * GROUP], scratch[2 * GROUP:]
    copies = fetch(
        [(x_u, values.at[LOW]), (hi_b, t0), (lo_a, t1), (u_h, t2), (m_h, t3), (w_h, t4)], sems
    )
    clear(sums)
    for copy in copies:
        copy.wait()
    values[HIGH, :] = A1 * (t3[...] * (t0[...] + t1[...]) + t4[...] * t2[...])
    add_elements(conn, scale, matrix, values, picked, local, sums)
    low_ref[...] = total(sums, 0)
    high_ref[...] = total(sums, HB)


def kernel_d(conn, scale, matrix, x_u, lo_a, hi_b, u_l, m_l, w_l, lo_c, u_u, m_u, w_u,
             low_ref, high_ref, sems, values, t0, t1, t2, t3, t4, t5, t6, t7, t8, *scratch):
    picked, local, sums = scratch[:GROUP], scratch[GROUP:2 * GROUP], scratch[2 * GROUP:]
    copies = fetch(
        [(x_u, values.at[HIGH]), (lo_a, t0), (hi_b, t1), (u_l, t2), (m_l, t3), (w_l, t4),
         (lo_c, t5), (u_u, t6), (m_u, t7), (w_u, t8)],
        sems,
    )
    clear(sums)
    for copy in copies[:6]:
        copy.wait()
    values[LOW, :] = A1 * (t3[...] * (t0[...] + t1[...]) + t4[...] * t2[...])
    add_elements(conn, scale, matrix, values, picked, local, sums)
    for copy in copies[6:]:
        copy.wait()
    low_ref[...] = A2 * (t3[...] * total(sums, 0) + t4[...] * values[LOW, :]) - A3 * t2[...]
    high_ref[...] = (
        A2 * (t7[...] * (t5[...] + total(sums, HB)) + t8[...] * values[HIGH, :]) - A3 * t6[...]
    )


def element_call(kernel, outs, temporaries, *operands):
    count = len(operands) - 3
    return pl.pallas_call(
        kernel,
        out_shape=(NODE_BLOCK,) * outs,
        in_specs=[SM, SM, VM] + [ANY] * count,
        out_specs=(VM,) * outs,
        scratch_shapes=[pltpu.SemaphoreType.DMA((count,)), pltpu.VMEM((2 * HB, LANES), F32)]
        + [pltpu.VMEM((HB, LANES), F32)] * temporaries
        + [pltpu.VMEM((LANES, LANES), F32)] * (2 * GROUP)
        + [pltpu.VMEM((2 * HB, LANES), F32)] * GROUP,
        compiler_params=PARAMS,
        cost_estimate=cost(13),
    )(*operands)


def spread_kernel(mass, well, *outs):
    count = HB // LANES
    for chunk in range(mass.shape[0]):
        rows = pl.ds(chunk % count * LANES, LANES)
        one = jnp.broadcast_to(mass[pl.ds(chunk, 1), :], (LANES, LANES))
        outs[chunk // count * 2][rows, :] = (one * one).T
        two = jnp.broadcast_to(well[pl.ds(chunk, 1), :] - CENTRE, (LANES, LANES))
        outs[chunk // count * 2 + 1][rows, :] = two.T


def spread(mass, well):
    outs = 2 * (mass.shape[0] * LANES // HB)
    return pl.pallas_call(
        spread_kernel,
        out_shape=(NODE_BLOCK,) * outs,
        in_specs=[VM, VM],
        out_specs=(VM,) * outs,
        compiler_params=PARAMS,
        cost_estimate=cost(outs),
    )(mass, well)


def enter_kernel(core, block, other, mass, low_ref, high_ref, mine, sem):
    owned = 2 * HB
    start = pl.multiple_of(core[0] * owned, owned)
    copy = pltpu.make_async_copy(block.at[:, pl.ds(start, owned)], mine, sem)
    copy.start()
    copy.wait()
    first = core[0] == 0
    for chunk in range(owned // LANES):
        columns = pl.ds(chunk * LANES, LANES)
        a, b = mine[:, columns], other[:, columns]
        stacked = jnp.concatenate([jnp.where(first, a, b), jnp.where(first, b, a)], axis=0)
        target = low_ref if chunk < HB // LANES else high_ref
        rows = pl.ds(chunk % (HB // LANES) * LANES, LANES)
        target[rows, :] = (stacked * mass[pl.ds(chunk, 1), :]).T


def enter(core, block, other, mass):
    return pl.pallas_call(
        enter_kernel,
        out_shape=(NODE_BLOCK, NODE_BLOCK),
        in_specs=[SM, ANY, VM, VM],
        out_specs=(VM, VM),
        scratch_shapes=[pltpu.VMEM((block.shape[0], 2 * HB), F32), pltpu.SemaphoreType.DMA],
        compiler_params=PARAMS,
        cost_estimate=cost(4),
    )(core, block, other, mass)


FINISH = 512


def finish_kernel(row, f_l, hi_c, m_l, f_u, mass, out_ref, away_ref):
    step = pl.program_id(0)
    count = FINISH // LANES
    for chunk in range(count):
        rows = pl.ds(chunk * LANES, LANES)
        turned = []
        for half in range(2):
            value = f_l[rows, :] + A2 * (m_l[rows, :] * hi_c[rows, :]) if half == 0 else f_u[rows, :]
            at = half * (HB // LANES) + step * count + chunk
            value = value.T / mass[pl.ds(at, 1), :]
            order = [
                value[kk * 4 * SB + c * SB:kk * 4 * SB + (c + 1) * SB, :]
                for c in range(4) for kk in range(2)
            ]
            value = jnp.concatenate(order, axis=0)
            turned.append(value)
            out_ref[half, chunk] = value
        away_ref[chunk] = jnp.where(row[0] == 0, turned[1], turned[0])


def finish(row, *operands):
    part = pl.BlockSpec((FINISH, LANES), lambda i: (i, 0))
    count = FINISH // LANES
    return pl.pallas_call(
        finish_kernel,
        out_shape=(
            jax.ShapeDtypeStruct((2, HB // LANES, LANES, LANES), F32),
            jax.ShapeDtypeStruct((HB // LANES, LANES, LANES), F32),
        ),
        grid=(HB // FINISH,),
        in_specs=[SM] + [part] * (len(operands) - 1) + [VM],
        out_specs=(
            pl.BlockSpec((2, count, LANES, LANES), lambda i: (0, i, 0, 0)),
            pl.BlockSpec((count, LANES, LANES), lambda i: (i, 0, 0)),
        ),
        compiler_params=PARAMS,
        cost_estimate=cost(3),
    )(row, *operands)


def overlap_kernel(weight, row, tiles, received, shares, mine, main, cross, panel, sem):
    copy = pltpu.make_async_copy(tiles.at[row[0]], mine, sem)
    copy.start()
    main[...] = jnp.zeros_like(main)
    cross[...] = jnp.zeros_like(cross)
    first = row[0] == 0
    copy.wait()

    @pl.loop(0, received.shape[0] // 2)
    def _(step):
        blocks = []
        for c in range(4):
            rows = pl.ds(c * 2 * SB, 2 * SB)
            a = jnp.concatenate([mine[2 * step, rows, :], mine[2 * step + 1, rows, :]], axis=1)
            b = jnp.concatenate(
                [received[2 * step, rows, :], received[2 * step + 1, rows, :]], axis=1
            )
            blocks += [jnp.where(first, a, b), jnp.where(first, b, a)]
        high, low = split(jnp.concatenate(blocks, axis=0))
        main[...] += dot_t(high, high)
        cross[...] += dot_t(high, low)

    panel[...] = (main[...] + (cross[...] + cross[...].T)) * weight
    for n in range(4 * SB // SHARE * 2):
        for c in range(4):
            shares[n * 4 + c] = panel[
                pl.ds(c * 4 * SB + n // 2 * SHARE, SHARE), pl.ds(n % 2 * LANES, LANES)
            ]


def overlap(weight, row, tiles, received):
    states = 2 * LANES
    return pl.pallas_call(
        functools.partial(overlap_kernel, weight),
        out_shape=jax.ShapeDtypeStruct((8 * tiles.shape[1], SHARE, LANES), F32),
        in_specs=[SM, ANY, VM],
        out_specs=VM,
        scratch_shapes=[pltpu.VMEM(tiles.shape[1:], F32)]
        + [pltpu.VMEM((states, states), F32)] * 3
        + [pltpu.SemaphoreType.DMA],
        compiler_params=PARAMS,
        cost_estimate=cost(5),
    )(row, tiles, received)


def place_kernel(moved, *refs):
    out_ref = refs[-1]
    for p in range(moved.shape[0] // 4):
        for y in range(2):
            for core in range(2):
                out_ref[pl.ds(y * 2 * SB, 2 * SB), pl.ds((2 * p + core) * NB, NB)] = moved[
                    p * 4 + y * 2 + core
                ]


def place(half, moved, *placed):
    steps, sources = 2, moved.shape[0]
    width = sources // 2 * NB // (2 * steps)
    return pl.pallas_call(
        place_kernel,
        out_shape=jax.ShapeDtypeStruct((4 * SB, sources // 2 * NB), F32),
        grid=(steps,),
        in_specs=[
            pl.BlockSpec(
                (sources // (2 * steps),) + moved.shape[1:], lambda i: (half * steps + i, 0, 0)
            )
        ] + [ANY] * len(placed),
        out_specs=pl.BlockSpec((4 * SB, width), lambda i: (0, half * steps + i)),
        input_output_aliases={1: 0} if placed else {},
        compiler_params=PARAMS,
        cost_estimate=cost(3),
    )(moved, *placed)


def shards(block, inv_sqrt_mass, potential, elem_scale, connectivity, elem_matrix):
    both = ("nodes", "grid")
    parts = lax.axis_size("nodes")
    grid = lax.axis_index("grid")
    row, core = grid // 2, grid % 2
    owned = 2 * HB

    def along(step):
        pairs = []
        for y in range(2):
            for source in range(2 * parts):
                target = source + step
                if 0 <= target < 2 * parts:
                    pairs.append((
                        source // 2 * 4 + y * 2 + source % 2,
                        target // 2 * 4 + y * 2 + target % 2,
                    ))
        return lambda value: lax.ppermute(value, both, pairs)

    to_previous, to_next = along(-1), along(1)

    other = lax.dynamic_slice(block, (0, (1 - core) * owned), (block.shape[0], owned))
    other = lax.ppermute(other, "grid", [(0, 1), (1, 0), (2, 3), (3, 2)])
    fields = jnp.stack([inv_sqrt_mass, potential]).reshape(2, -1, LANES)
    count = HB // LANES
    rim = lax.ppermute(fields[:, :count], "nodes", [(n, n - 1) for n in range(1, parts)])
    own = lax.dynamic_slice(fields, (0, core * 2 * count, 0), (2, 2 * count, LANES))
    m_l, w_l, m_u, w_u = spread(own[0], own[1])

    conn = lax.dynamic_slice(connectivity, (core * 2 * EL, 0), (2 * EL, NPE)) - core * owned
    conn = jnp.pad(conn, ((0, 0), (0, LANES - NPE)))
    c_l, c_u = conn[:EL].reshape(-1), (conn[EL:] - HB).reshape(-1)
    scale = lax.dynamic_slice(elem_scale, (core * 2 * EL,), (2 * EL,))
    s_l, s_u = scale[:EL], scale[EL:]
    matrix = jnp.pad(elem_matrix, ((0, LANES - NPE), (0, LANES - NPE)))

    u_l, u_u = enter(core[None], block, other, own[0])
    u_h = to_previous(u_l)
    a_l, rim = lax.optimization_barrier((u_l, rim))
    last = jnp.where(core == 0, fields[:, 2 * count:3 * count], rim)
    lo_a, hi_a = element_call(kernel_a, 2, 0, c_l, s_l, matrix, a_l, u_u)
    lo_a_next = to_previous(lo_a)
    m_h, w_h = spread(last[0], last[1])
    x_u, hi_b = element_call(kernel_b, 2, 3, c_u, s_u, matrix, u_u, u_h, hi_a, m_u, w_u)
    hi_b_previous = to_next(hi_b)
    lo_c, hi_c = element_call(
        kernel_c, 2, 5, c_u, s_u, matrix, x_u, hi_b, lo_a_next, u_h, m_h, w_h
    )
    hi_c_previous = to_next(hi_c)
    f_l, f_u = element_call(
        kernel_d, 2, 9, c_l, s_l, matrix,
        x_u, lo_a, hi_b_previous, u_l, m_l, w_l, lo_c, u_u, m_u, w_u,
    )
    tiles, away = finish(row[None], f_l, hi_c_previous, m_l, f_u, own[0])
    received = lax.ppermute(away, "grid", [(0, 2), (1, 3), (2, 0), (3, 1)])

    moved = lax.all_to_all(
        tiles.reshape(4 * parts, 2 * SB, NB), both, split_axis=0, concat_axis=0, tiled=True
    )
    shares = overlap(1.0 / (parts * 4 * HB), row[None], tiles, received)
    moved, shares = lax.optimization_barrier((moved, shares))
    shares = lax.all_to_all(shares, both, split_axis=0, concat_axis=0, tiled=True)
    cyclic = place(0, moved)
    share = jnp.sum(shares, axis=0)
    share, moved, cyclic = lax.optimization_barrier((share, moved, cyclic))
    shares = lax.all_to_all(
        jnp.broadcast_to(share[None], (parts, SHARE, LANES)),
        "nodes", split_axis=0, concat_axis=0, tiled=True,
    )
    cyclic = place(1, moved, cyclic)
    rows = shares.reshape(parts // 2, 2, SHARE, LANES).transpose(0, 2, 1, 3)
    intersection = rows.reshape(4 * SB, 2 * LANES).T
    return (cyclic, intersection)


def solution(mesh):
    placed = (P("grid", "nodes"), P("nodes"), P("nodes"), P("nodes"), P("nodes", None), P())
    return jax.shard_map(
        shards,
        mesh=mesh,
        in_specs=placed,
        out_specs=(P("grid", "nodes"), P(None, "grid")),
        check_vma=False,
    )
```

```python
import functools

import jax
import jax.numpy as jnp
from jax import lax
from jax.experimental import pallas as pl
from jax.experimental.pallas import tpu as pltpu
from jax.sharding import PartitionSpec as P

F32, BF16 = jnp.float32, jnp.bfloat16
HB = 2048
LANES = 128
NPE = 125
EL = 32
STRIDE = 64
GROUP = 8
NB, SB = 128, 16

LOWEST, CUT, TOP = -2.0, 4.0, 32.0
HALF = (TOP - CUT) / 2.0
CENTRE = (TOP + CUT) / 2.0
SIGMA = HALF / (LOWEST - CENTRE)
SIGMA_TWO = 1.0 / (2.0 / SIGMA - SIGMA)
A1 = SIGMA / HALF
A2 = 2.0 * SIGMA_TWO / HALF
A3 = SIGMA * SIGMA_TWO

VM = pl.BlockSpec(memory_space=pltpu.VMEM)
SM = pl.BlockSpec(memory_space=pltpu.SMEM)
ANY = pl.BlockSpec(memory_space=pl.ANY)
NODE_BLOCK = jax.ShapeDtypeStruct((HB, LANES), F32)
PARAMS = pltpu.CompilerParams(vmem_limit_bytes=40 << 20)
LARGE = pltpu.CompilerParams(vmem_limit_bytes=56 << 20)
SHARE = 4


def split(value):
    high = value.astype(BF16)
    return high, (value - high.astype(F32)).astype(BF16)


def dot(a, b):
    return lax.dot_general(a, b, (((1,), (0,)), ((), ())), preferred_element_type=F32)


def dot_t(a, b):
    return lax.dot_general(a, b, (((1,), (1,)), ((), ())), preferred_element_type=F32)


def cost(microseconds):
    return pl.CostEstimate(flops=0, transcendentals=0, bytes_accessed=int(microseconds * 3.0e6))


RUN = EL // GROUP
REACH = 2304
PIECE = 256


def clear(sums):
    for k, ref in enumerate(sums):
        start = k * RUN * STRIDE
        size = min(REACH, 2 * HB - start)
        ref[pl.ds(start, size), :] = jnp.zeros((size, LANES), F32)


def add_elements(conn, scale, matrix, values, picked, local, sums):
    high, low = split(matrix[...])
    left = jnp.concatenate(
        [
            jnp.concatenate([high, high], axis=1),
            jnp.concatenate([low, jnp.zeros_like(low)], axis=1),
        ],
        axis=0,
    )
    for ref in picked:
        ref[pl.ds(NPE, LANES - NPE), :] = jnp.zeros((LANES - NPE, LANES), F32)

    @pl.loop(0, RUN)
    def _(step):
        base = step * LANES
        for i in range(NPE):
            for k in range(GROUP):
                node = conn[base + (k * RUN * LANES + i)]
                picked[k][pl.ds(i, 1), :] = values[pl.ds(node, 1), :]
        for k in range(0, GROUP, 2):
            pair = [split(picked[k + j][...]) for j in range(2)]
            right = jnp.concatenate(
                [
                    jnp.concatenate([pair[0][0], pair[1][0]], axis=1),
                    jnp.concatenate([pair[0][1], pair[1][1]], axis=1),
                ],
                axis=0,
            )
            product = dot(left, right)
            product = product[:LANES] + product[LANES:]
            for j in range(2):
                local[k + j][...] = (
                    product[:, j * LANES:(j + 1) * LANES] * scale[step + (k + j) * RUN]
                )
        for i in range(NPE):
            for k in range(GROUP):
                node = conn[base + (k * RUN * LANES + i)]
                row = pl.ds(node, 1)
                sums[k][row, :] = sums[k][row, :] + local[k][pl.ds(i, 1), :]


def total(sums, start):
    pieces = []
    for row in range(start, start + HB, PIECE):
        parts = [
            ref[pl.ds(row, PIECE), :]
            for k, ref in enumerate(sums)
            if 0 <= row - k * RUN * STRIDE < REACH
        ]
        while len(parts) > 1:
            parts = [a + b for a, b in zip(parts[::2], parts[1::2])] + (
                [parts[-1]] if len(parts) % 2 else []
            )
        pieces.append(parts[0])
    return jnp.concatenate(pieces, axis=0)


def fetch(pairs, sems):
    copies = [
        pltpu.make_async_copy(source, target, sems.at[i])
        for i, (source, target) in enumerate(pairs)
    ]
    for copy in copies:
        copy.start()
    return copies


LOW, HIGH = pl.ds(0, HB), pl.ds(HB, HB)


def kernel_a(conn, scale, matrix, u_l, u_u, low_ref, high_ref, sems, values, *scratch):
    picked, local, sums = scratch[:GROUP], scratch[GROUP:2 * GROUP], scratch[2 * GROUP:]
    copies = fetch([(u_l, values.at[LOW]), (u_u, values.at[HIGH])], sems)
    clear(sums)
    for copy in copies:
        copy.wait()
    add_elements(conn, scale, matrix, values, picked, local, sums)
    low_ref[...] = total(sums, 0)
    high_ref[...] = total(sums, HB)


def kernel_b(conn, scale, matrix, u_u, u_h, hi_a, m_u, w_u, x_ref, high_ref,
             sems, values, t0, t1, t2, *scratch):
    picked, local, sums = scratch[:GROUP], scratch[GROUP:2 * GROUP], scratch[2 * GROUP:]
    copies = fetch(
        [(u_u, values.at[LOW]), (u_h, values.at[HIGH]), (hi_a, t0), (m_u, t1), (w_u, t2)], sems
    )
    clear(sums)
    for copy in copies:
        copy.wait()
    add_elements(conn, scale, matrix, values, picked, local, sums)
    x_ref[...] = A1 * (t1[...] * (t0[...] + total(sums, 0)) + t2[...] * values[LOW, :])
    high_ref[...] = total(sums, HB)


def kernel_c(conn, scale, matrix, x_u, hi_b, lo_a, u_h, m_h, w_h, low_ref, high_ref,
             sems, values, t0, t1, t2, t3, t4, *scratch):
    picked, local, sums = scratch[:GROUP], scratch[GROUP:2 * GROUP], scratch[2 * GROUP:]
    copies = fetch(
        [(x_u, values.at[LOW]), (hi_b, t0), (lo_a, t1), (u_h, t2), (m_h, t3), (w_h, t4)], sems
    )
    clear(sums)
    for copy in copies:
        copy.wait()
    values[HIGH, :] = A1 * (t3[...] * (t0[...] + t1[...]) + t4[...] * t2[...])
    add_elements(conn, scale, matrix, values, picked, local, sums)
    low_ref[...] = total(sums, 0)
    high_ref[...] = total(sums, HB)


def kernel_d(conn, scale, matrix, x_u, lo_a, hi_b, u_l, m_l, w_l, lo_c, u_u, m_u, w_u,
             low_ref, high_ref, sems, values, t0, t1, t2, t3, t4, t5, t6, t7, t8, *scratch):
    picked, local, sums = scratch[:GROUP], scratch[GROUP:2 * GROUP], scratch[2 * GROUP:]
    copies = fetch(
        [(x_u, values.at[HIGH]), (lo_a, t0), (hi_b, t1), (u_l, t2), (m_l, t3), (w_l, t4),
         (lo_c, t5), (u_u, t6), (m_u, t7), (w_u, t8)],
        sems,
    )
    clear(sums)
    for copy in copies[:6]:
        copy.wait()
    values[LOW, :] = A1 * (t3[...] * (t0[...] + t1[...]) + t4[...] * t2[...])
    add_elements(conn, scale, matrix, values, picked, local, sums)
    for copy in copies[6:]:
        copy.wait()
    low_ref[...] = A2 * (t3[...] * total(sums, 0) + t4[...] * values[LOW, :]) - A3 * t2[...]
    high_ref[...] = (
        A2 * (t7[...] * (t5[...] + total(sums, HB)) + t8[...] * values[HIGH, :]) - A3 * t6[...]
    )


def element_call(kernel, outs, temporaries, *operands, params=PARAMS):
    count = len(operands) - 3
    return pl.pallas_call(
        kernel,
        out_shape=(NODE_BLOCK,) * outs,
        in_specs=[SM, SM, VM] + [ANY] * count,
        out_specs=(VM,) * outs,
        scratch_shapes=[pltpu.SemaphoreType.DMA((count,)), pltpu.VMEM((2 * HB, LANES), F32)]
        + [pltpu.VMEM((HB, LANES), F32)] * temporaries
        + [pltpu.VMEM((LANES, LANES), F32)] * (2 * GROUP)
        + [pltpu.VMEM((2 * HB, LANES), F32)] * GROUP,
        compiler_params=params,
        cost_estimate=cost(13),
    )(*operands)


def spread_kernel(mass, well, *outs):
    count = HB // LANES
    for chunk in range(mass.shape[0]):
        rows = pl.ds(chunk % count * LANES, LANES)
        one = jnp.broadcast_to(mass[pl.ds(chunk, 1), :], (LANES, LANES))
        outs[chunk // count * 2][rows, :] = (one * one).T
        two = jnp.broadcast_to(well[pl.ds(chunk, 1), :] - CENTRE, (LANES, LANES))
        outs[chunk // count * 2 + 1][rows, :] = two.T


def spread(mass, well):
    outs = 2 * (mass.shape[0] * LANES // HB)
    return pl.pallas_call(
        spread_kernel,
        out_shape=(NODE_BLOCK,) * outs,
        in_specs=[VM, VM],
        out_specs=(VM,) * outs,
        compiler_params=PARAMS,
        cost_estimate=cost(outs),
    )(mass, well)


def enter_kernel(core, block, other, mass, low_ref, high_ref, mine, sem):
    owned = 2 * HB
    start = pl.multiple_of(core[0] * owned, owned)
    copy = pltpu.make_async_copy(block.at[:, pl.ds(start, owned)], mine, sem)
    copy.start()
    copy.wait()
    first = core[0] == 0
    for chunk in range(owned // LANES):
        columns = pl.ds(chunk * LANES, LANES)
        a, b = mine[:, columns], other[:, columns]
        stacked = jnp.concatenate([jnp.where(first, a, b), jnp.where(first, b, a)], axis=0)
        target = low_ref if chunk < HB // LANES else high_ref
        rows = pl.ds(chunk % (HB // LANES) * LANES, LANES)
        target[rows, :] = (stacked * mass[pl.ds(chunk, 1), :]).T


def enter(core, block, other, mass):
    return pl.pallas_call(
        enter_kernel,
        out_shape=(NODE_BLOCK, NODE_BLOCK),
        in_specs=[SM, ANY, VM, VM],
        out_specs=(VM, VM),
        scratch_shapes=[pltpu.VMEM((block.shape[0], 2 * HB), F32), pltpu.SemaphoreType.DMA],
        compiler_params=PARAMS,
        cost_estimate=cost(4),
    )(core, block, other, mass)


FINISH = 512


def finish_kernel(row, f_l, hi_c, m_l, f_u, mass, out_ref, away_ref):
    step = pl.program_id(0)
    count = FINISH // LANES
    for chunk in range(count):
        rows = pl.ds(chunk * LANES, LANES)
        turned = []
        for half in range(2):
            value = f_l[rows, :] + A2 * (m_l[rows, :] * hi_c[rows, :]) if half == 0 else f_u[rows, :]
            at = half * (HB // LANES) + step * count + chunk
            value = value.T / mass[pl.ds(at, 1), :]
            order = [
                value[kk * 4 * SB + c * SB:kk * 4 * SB + (c + 1) * SB, :]
                for c in range(4) for kk in range(2)
            ]
            value = jnp.concatenate(order, axis=0)
            turned.append(value)
            out_ref[half, chunk] = value
        away_ref[chunk] = jnp.where(row[0] == 0, turned[1], turned[0])


def finish(row, *operands):
    part = pl.BlockSpec((FINISH, LANES), lambda i: (i, 0))
    count = FINISH // LANES
    return pl.pallas_call(
        finish_kernel,
        out_shape=(
            jax.ShapeDtypeStruct((2, HB // LANES, LANES, LANES), F32),
            jax.ShapeDtypeStruct((HB // LANES, LANES, LANES), F32),
        ),
        grid=(HB // FINISH,),
        in_specs=[SM] + [part] * (len(operands) - 1) + [VM],
        out_specs=(
            pl.BlockSpec((2, count, LANES, LANES), lambda i: (0, i, 0, 0)),
            pl.BlockSpec((count, LANES, LANES), lambda i: (i, 0, 0)),
        ),
        compiler_params=PARAMS,
        cost_estimate=cost(3),
    )(row, *operands)


def overlap_kernel(weight, row, tiles, received, shares, mine, main, cross, panel, sem):
    copy = pltpu.make_async_copy(tiles.at[row[0]], mine, sem)
    copy.start()
    main[...] = jnp.zeros_like(main)
    cross[...] = jnp.zeros_like(cross)
    first = row[0] == 0
    copy.wait()

    @pl.loop(0, received.shape[0] // 2)
    def _(step):
        blocks = []
        for c in range(4):
            rows = pl.ds(c * 2 * SB, 2 * SB)
            a = jnp.concatenate([mine[2 * step, rows, :], mine[2 * step + 1, rows, :]], axis=1)
            b = jnp.concatenate(
                [received[2 * step, rows, :], received[2 * step + 1, rows, :]], axis=1
            )
            blocks += [jnp.where(first, a, b), jnp.where(first, b, a)]
        high, low = split(jnp.concatenate(blocks, axis=0))
        main[...] += dot_t(high, high)
        cross[...] += dot_t(high, low)

    panel[...] = (main[...] + (cross[...] + cross[...].T)) * weight
    for n in range(4 * SB // SHARE * 2):
        for c in range(4):
            shares[n * 4 + c] = panel[
                pl.ds(c * 4 * SB + n // 2 * SHARE, SHARE), pl.ds(n % 2 * LANES, LANES)
            ]


def overlap(weight, row, tiles, received):
    states = 2 * LANES
    return pl.pallas_call(
        functools.partial(overlap_kernel, weight),
        out_shape=jax.ShapeDtypeStruct((8 * tiles.shape[1], SHARE, LANES), F32),
        in_specs=[SM, ANY, VM],
        out_specs=VM,
        scratch_shapes=[pltpu.VMEM(tiles.shape[1:], F32)]
        + [pltpu.VMEM((states, states), F32)] * 3
        + [pltpu.SemaphoreType.DMA],
        compiler_params=PARAMS,
        cost_estimate=cost(5),
    )(row, tiles, received)


def place_kernel(moved, *refs):
    out_ref = refs[-1]
    for p in range(moved.shape[0] // 4):
        for y in range(2):
            for core in range(2):
                out_ref[pl.ds(y * 2 * SB, 2 * SB), pl.ds((2 * p + core) * NB, NB)] = moved[
                    p * 4 + y * 2 + core
                ]


def place(half, moved, *placed):
    steps, sources = 2, moved.shape[0]
    width = sources // 2 * NB // (2 * steps)
    return pl.pallas_call(
        place_kernel,
        out_shape=jax.ShapeDtypeStruct((4 * SB, sources // 2 * NB), F32),
        grid=(steps,),
        in_specs=[
            pl.BlockSpec(
                (sources // (2 * steps),) + moved.shape[1:], lambda i: (half * steps + i, 0, 0)
            )
        ] + [ANY] * len(placed),
        out_specs=pl.BlockSpec((4 * SB, width), lambda i: (0, half * steps + i)),
        input_output_aliases={1: 0} if placed else {},
        compiler_params=PARAMS,
        cost_estimate=cost(3),
    )(moved, *placed)


def shards(block, inv_sqrt_mass, potential, elem_scale, connectivity, elem_matrix):
    both = ("nodes", "grid")
    parts = lax.axis_size("nodes")
    grid = lax.axis_index("grid")
    row, core = grid // 2, grid % 2
    owned = 2 * HB

    def along(step):
        pairs = []
        for y in range(2):
            for source in range(2 * parts):
                target = source + step
                if 0 <= target < 2 * parts:
                    pairs.append((
                        source // 2 * 4 + y * 2 + source % 2,
                        target // 2 * 4 + y * 2 + target % 2,
                    ))
        return lambda value: lax.ppermute(value, both, pairs)

    to_previous, to_next = along(-1), along(1)

    other = lax.dynamic_slice(block, (0, (1 - core) * owned), (block.shape[0], owned))
    other = lax.ppermute(other, "grid", [(0, 1), (1, 0), (2, 3), (3, 2)])
    fields = jnp.stack([inv_sqrt_mass, potential]).reshape(2, -1, LANES)
    count = HB // LANES
    rim = lax.ppermute(fields[:, :count], "nodes", [(n, n - 1) for n in range(1, parts)])
    own = lax.dynamic_slice(fields, (0, core * 2 * count, 0), (2, 2 * count, LANES))
    m_l, w_l, m_u, w_u = spread(own[0], own[1])

    conn = lax.dynamic_slice(connectivity, (core * 2 * EL, 0), (2 * EL, NPE)) - core * owned
    conn = jnp.pad(conn, ((0, 0), (0, LANES - NPE)))
    c_l, c_u = conn[:EL].reshape(-1), (conn[EL:] - HB).reshape(-1)
    scale = lax.dynamic_slice(elem_scale, (core * 2 * EL,), (2 * EL,))
    s_l, s_u = scale[:EL], scale[EL:]
    matrix = jnp.pad(elem_matrix, ((0, LANES - NPE), (0, LANES - NPE)))

    u_l, u_u = enter(core[None], block, other, own[0])
    u_h = to_previous(u_l)
    a_l, rim = lax.optimization_barrier((u_l, rim))
    last = jnp.where(core == 0, fields[:, 2 * count:3 * count], rim)
    lo_a, hi_a = element_call(kernel_a, 2, 0, c_l, s_l, matrix, a_l, u_u)
    lo_a_next = to_previous(lo_a)
    m_h, w_h = spread(last[0], last[1])
    x_u, hi_b = element_call(kernel_b, 2, 3, c_u, s_u, matrix, u_u, u_h, hi_a, m_u, w_u)
    hi_b_previous = to_next(hi_b)
    lo_c, hi_c = element_call(
        kernel_c, 2, 5, c_u, s_u, matrix, x_u, hi_b, lo_a_next, u_h, m_h, w_h
    )
    hi_c_previous = to_next(hi_c)
    f_l, f_u = element_call(
        kernel_d, 2, 9, c_l, s_l, matrix,
        x_u, lo_a, hi_b_previous, u_l, m_l, w_l, lo_c, u_u, m_u, w_u, params=LARGE,
    )
    tiles, away = finish(row[None], f_l, hi_c_previous, m_l, f_u, own[0])
    received = lax.ppermute(away, "grid", [(0, 2), (1, 3), (2, 0), (3, 1)])

    moved = lax.all_to_all(
        tiles.reshape(4 * parts, 2 * SB, NB), both, split_axis=0, concat_axis=0, tiled=True
    )
    shares = overlap(1.0 / (parts * 4 * HB), row[None], tiles, received)
    moved, shares = lax.optimization_barrier((moved, shares))
    shares = lax.all_to_all(shares, both, split_axis=0, concat_axis=0, tiled=True)
    cyclic = place(0, moved)
    share = jnp.sum(shares, axis=0)
    share, moved, cyclic = lax.optimization_barrier((share, moved, cyclic))
    shares = lax.all_to_all(
        jnp.broadcast_to(share[None], (parts, SHARE, LANES)),
        "nodes", split_axis=0, concat_axis=0, tiled=True,
    )
    cyclic = place(1, moved, cyclic)
    rows = shares.reshape(parts // 2, 2, SHARE, LANES).transpose(0, 2, 1, 3)
    intersection = rows.reshape(4 * SB, 2 * LANES).T
    return (cyclic, intersection)


def solution(mesh):
    placed = (P("grid", "nodes"), P("nodes"), P("nodes"), P("nodes"), P("nodes", None), P())
    return jax.shard_map(
        shards,
        mesh=mesh,
        in_specs=placed,
        out_specs=(P("grid", "nodes"), P(None, "grid")),
        check_vma=False,
    )
```

```python
import functools

import jax
import jax.numpy as jnp
from jax import lax
from jax.experimental import pallas as pl
from jax.experimental.pallas import tpu as pltpu
from jax.sharding import PartitionSpec as P

F32, BF16 = jnp.float32, jnp.bfloat16
HB = 2048
LANES = 128
NPE = 125
EL = 32
STRIDE = 64
GROUP = 8
NB, SB = 128, 16

LOWEST, CUT, TOP = -2.0, 4.0, 32.0
HALF = (TOP - CUT) / 2.0
CENTRE = (TOP + CUT) / 2.0
SIGMA = HALF / (LOWEST - CENTRE)
SIGMA_TWO = 1.0 / (2.0 / SIGMA - SIGMA)
A1 = SIGMA / HALF
A2 = 2.0 * SIGMA_TWO / HALF
A3 = SIGMA * SIGMA_TWO

VM = pl.BlockSpec(memory_space=pltpu.VMEM)
SM = pl.BlockSpec(memory_space=pltpu.SMEM)
ANY = pl.BlockSpec(memory_space=pl.ANY)
NODE_BLOCK = jax.ShapeDtypeStruct((HB, LANES), F32)
PARAMS = pltpu.CompilerParams(vmem_limit_bytes=40 << 20)
LARGE = pltpu.CompilerParams(vmem_limit_bytes=56 << 20)
SHARE = 4


def split(value):
    high = value.astype(BF16)
    return high, (value - high.astype(F32)).astype(BF16)


def dot(a, b):
    return lax.dot_general(a, b, (((1,), (0,)), ((), ())), preferred_element_type=F32)


def dot_t(a, b):
    return lax.dot_general(a, b, (((1,), (1,)), ((), ())), preferred_element_type=F32)


def cost(microseconds):
    return pl.CostEstimate(flops=0, transcendentals=0, bytes_accessed=int(microseconds * 3.0e6))


RUN = EL // GROUP
REACH = 2304
PIECE = 256


def clear(sums):
    for k, ref in enumerate(sums):
        start = k * RUN * STRIDE
        size = min(REACH, 2 * HB - start)
        ref[pl.ds(start, size), :] = jnp.zeros((size, LANES), F32)


def add_elements(conn, scale, matrix, values, picked, local, sums):
    high, low = split(matrix[...])
    left = jnp.concatenate(
        [
            jnp.concatenate([high, high], axis=1),
            jnp.concatenate([low, jnp.zeros_like(low)], axis=1),
        ],
        axis=0,
    )
    for ref in picked:
        ref[pl.ds(NPE, LANES - NPE), :] = jnp.zeros((LANES - NPE, LANES), F32)

    @pl.loop(0, RUN)
    def _(step):
        base = step * LANES
        for i in range(NPE):
            for k in range(GROUP):
                node = conn[base + (k * RUN * LANES + i)]
                picked[k][pl.ds(i, 1), :] = values[pl.ds(node, 1), :]
        for k in range(0, GROUP, 2):
            pair = [split(picked[k + j][...]) for j in range(2)]
            right = jnp.concatenate(
                [
                    jnp.concatenate([pair[0][0], pair[1][0]], axis=1),
                    jnp.concatenate([pair[0][1], pair[1][1]], axis=1),
                ],
                axis=0,
            )
            product = dot(left, right)
            product = product[:LANES] + product[LANES:]
            for j in range(2):
                local[k + j][...] = (
                    product[:, j * LANES:(j + 1) * LANES] * scale[step + (k + j) * RUN]
                )
        for i in range(NPE):
            for k in range(GROUP):
                node = conn[base + (k * RUN * LANES + i)]
                row = pl.ds(node, 1)
                sums[k][row, :] = sums[k][row, :] + local[k][pl.ds(i, 1), :]


def total(sums, start):
    pieces = []
    for row in range(start, start + HB, PIECE):
        parts = [
            ref[pl.ds(row, PIECE), :]
            for k, ref in enumerate(sums)
            if 0 <= row - k * RUN * STRIDE < REACH
        ]
        while len(parts) > 1:
            parts = [a + b for a, b in zip(parts[::2], parts[1::2])] + (
                [parts[-1]] if len(parts) % 2 else []
            )
        pieces.append(parts[0])
    return jnp.concatenate(pieces, axis=0)


def fetch(pairs, sems):
    copies = [
        pltpu.make_async_copy(source, target, sems.at[i])
        for i, (source, target) in enumerate(pairs)
    ]
    for copy in copies:
        copy.start()
    return copies


LOW, HIGH = pl.ds(0, HB), pl.ds(HB, HB)


def kernel_a(conn, scale, matrix, u_l, u_u, low_ref, high_ref, sems, values, *scratch):
    picked, local, sums = scratch[:GROUP], scratch[GROUP:2 * GROUP], scratch[2 * GROUP:]
    copies = fetch([(u_l, values.at[LOW]), (u_u, values.at[HIGH])], sems)
    clear(sums)
    for copy in copies:
        copy.wait()
    add_elements(conn, scale, matrix, values, picked, local, sums)
    low_ref[...] = total(sums, 0)
    high_ref[...] = total(sums, HB)


def kernel_b(conn, scale, matrix, u_u, u_h, hi_a, m_u, w_u, x_ref, high_ref,
             sems, values, t0, t1, t2, *scratch):
    picked, local, sums = scratch[:GROUP], scratch[GROUP:2 * GROUP], scratch[2 * GROUP:]
    copies = fetch(
        [(u_u, values.at[LOW]), (u_h, values.at[HIGH]), (hi_a, t0), (m_u, t1), (w_u, t2)], sems
    )
    clear(sums)
    for copy in copies:
        copy.wait()
    add_elements(conn, scale, matrix, values, picked, local, sums)
    x_ref[...] = A1 * (t1[...] * (t0[...] + total(sums, 0)) + t2[...] * values[LOW, :])
    high_ref[...] = total(sums, HB)


def kernel_c(conn, scale, matrix, x_u, hi_b, lo_a, u_h, m_h, w_h, low_ref, high_ref,
             sems, values, t0, t1, t2, t3, t4, *scratch):
    picked, local, sums = scratch[:GROUP], scratch[GROUP:2 * GROUP], scratch[2 * GROUP:]
    copies = fetch(
        [(x_u, values.at[LOW]), (hi_b, t0), (lo_a, t1), (u_h, t2), (m_h, t3), (w_h, t4)], sems
    )
    clear(sums)
    for copy in copies:
        copy.wait()
    values[HIGH, :] = A1 * (t3[...] * (t0[...] + t1[...]) + t4[...] * t2[...])
    add_elements(conn, scale, matrix, values, picked, local, sums)
    low_ref[...] = total(sums, 0)
    high_ref[...] = total(sums, HB)


def kernel_d(conn, scale, matrix, x_u, lo_a, hi_b, u_l, m_l, w_l, lo_c, u_u, m_u, w_u,
             low_ref, high_ref, sems, values, t0, t1, t2, t3, t4, t5, t6, t7, t8, *scratch):
    picked, local, sums = scratch[:GROUP], scratch[GROUP:2 * GROUP], scratch[2 * GROUP:]
    copies = fetch(
        [(x_u, values.at[HIGH]), (lo_a, t0), (hi_b, t1), (u_l, t2), (m_l, t3), (w_l, t4),
         (lo_c, t5), (u_u, t6), (m_u, t7), (w_u, t8)],
        sems,
    )
    clear(sums)
    for copy in copies[:6]:
        copy.wait()
    values[LOW, :] = A1 * (t3[...] * (t0[...] + t1[...]) + t4[...] * t2[...])
    add_elements(conn, scale, matrix, values, picked, local, sums)
    for copy in copies[6:]:
        copy.wait()
    low_ref[...] = A2 * (t3[...] * total(sums, 0) + t4[...] * values[LOW, :]) - A3 * t2[...]
    high_ref[...] = (
        A2 * (t7[...] * (t5[...] + total(sums, HB)) + t8[...] * values[HIGH, :]) - A3 * t6[...]
    )


def element_call(kernel, outs, temporaries, *operands, params=PARAMS):
    count = len(operands) - 3
    return pl.pallas_call(
        kernel,
        out_shape=(NODE_BLOCK,) * outs,
        in_specs=[SM, SM, VM] + [ANY] * count,
        out_specs=(VM,) * outs,
        scratch_shapes=[pltpu.SemaphoreType.DMA((count,)), pltpu.VMEM((2 * HB, LANES), F32)]
        + [pltpu.VMEM((HB, LANES), F32)] * temporaries
        + [pltpu.VMEM((LANES, LANES), F32)] * (2 * GROUP)
        + [pltpu.VMEM((2 * HB, LANES), F32)] * GROUP,
        compiler_params=params,
        cost_estimate=cost(13),
    )(*operands)


def spread_kernel(mass, well, *outs):
    count = HB // LANES
    for chunk in range(mass.shape[0]):
        rows = pl.ds(chunk % count * LANES, LANES)
        one = jnp.broadcast_to(mass[pl.ds(chunk, 1), :], (LANES, LANES))
        outs[chunk // count * 2][rows, :] = (one * one).T
        two = jnp.broadcast_to(well[pl.ds(chunk, 1), :] - CENTRE, (LANES, LANES))
        outs[chunk // count * 2 + 1][rows, :] = two.T


def spread(mass, well):
    outs = 2 * (mass.shape[0] * LANES // HB)
    return pl.pallas_call(
        spread_kernel,
        out_shape=(NODE_BLOCK,) * outs,
        in_specs=[VM, VM],
        out_specs=(VM,) * outs,
        compiler_params=PARAMS,
        cost_estimate=cost(outs),
    )(mass, well)


def enter_kernel(core, block, other, mass, low_ref, high_ref, mine, sem):
    owned = 2 * HB
    start = pl.multiple_of(core[0] * owned, owned)
    copy = pltpu.make_async_copy(block.at[:, pl.ds(start, owned)], mine, sem)
    copy.start()
    copy.wait()
    first = core[0] == 0
    for chunk in range(owned // LANES):
        columns = pl.ds(chunk * LANES, LANES)
        a, b = mine[:, columns], other[:, columns]
        stacked = jnp.concatenate([jnp.where(first, a, b), jnp.where(first, b, a)], axis=0)
        target = low_ref if chunk < HB // LANES else high_ref
        rows = pl.ds(chunk % (HB // LANES) * LANES, LANES)
        target[rows, :] = (stacked * mass[pl.ds(chunk, 1), :]).T


def enter(core, block, other, mass):
    return pl.pallas_call(
        enter_kernel,
        out_shape=(NODE_BLOCK, NODE_BLOCK),
        in_specs=[SM, ANY, VM, VM],
        out_specs=(VM, VM),
        scratch_shapes=[pltpu.VMEM((block.shape[0], 2 * HB), F32), pltpu.SemaphoreType.DMA],
        compiler_params=PARAMS,
        cost_estimate=cost(4),
    )(core, block, other, mass)


FINISH = 512


def finish_kernel(row, f_l, hi_c, m_l, f_u, mass, out_ref, away_ref):
    step = pl.program_id(0)
    count = FINISH // LANES
    for chunk in range(count):
        rows = pl.ds(chunk * LANES, LANES)
        turned = []
        for half in range(2):
            value = f_l[rows, :] + A2 * (m_l[rows, :] * hi_c[rows, :]) if half == 0 else f_u[rows, :]
            at = half * (HB // LANES) + step * count + chunk
            value = value.T / mass[pl.ds(at, 1), :]
            order = [
                value[kk * 4 * SB + c * SB:kk * 4 * SB + (c + 1) * SB, :]
                for c in range(4) for kk in range(2)
            ]
            value = jnp.concatenate(order, axis=0)
            turned.append(value)
            out_ref[half, chunk] = value
        away_ref[chunk] = jnp.where(row[0] == 0, turned[1], turned[0])


def finish(row, *operands):
    part = pl.BlockSpec((FINISH, LANES), lambda i: (i, 0))
    count = FINISH // LANES
    return pl.pallas_call(
        finish_kernel,
        out_shape=(
            jax.ShapeDtypeStruct((2, HB // LANES, LANES, LANES), F32),
            jax.ShapeDtypeStruct((HB // LANES, LANES, LANES), F32),
        ),
        grid=(HB // FINISH,),
        in_specs=[SM] + [part] * (len(operands) - 1) + [VM],
        out_specs=(
            pl.BlockSpec((2, count, LANES, LANES), lambda i: (0, i, 0, 0)),
            pl.BlockSpec((count, LANES, LANES), lambda i: (i, 0, 0)),
        ),
        compiler_params=PARAMS,
        cost_estimate=cost(3),
    )(row, *operands)


def overlap_kernel(weight, row, tiles, received, shares, mine, main, cross, panel, sem):
    copy = pltpu.make_async_copy(tiles.at[row[0]], mine, sem)
    copy.start()
    main[...] = jnp.zeros_like(main)
    cross[...] = jnp.zeros_like(cross)
    first = row[0] == 0
    copy.wait()

    @pl.loop(0, received.shape[0] // 2)
    def _(step):
        blocks = []
        for c in range(4):
            rows = pl.ds(c * 2 * SB, 2 * SB)
            a = jnp.concatenate([mine[2 * step, rows, :], mine[2 * step + 1, rows, :]], axis=1)
            b = jnp.concatenate(
                [received[2 * step, rows, :], received[2 * step + 1, rows, :]], axis=1
            )
            blocks += [jnp.where(first, a, b), jnp.where(first, b, a)]
        high, low = split(jnp.concatenate(blocks, axis=0))
        main[...] += dot_t(high, high)
        cross[...] += dot_t(high, low)

    panel[...] = (main[...] + (cross[...] + cross[...].T)) * weight
    for n in range(4 * SB // SHARE * 2):
        for c in range(4):
            shares[n * 4 + c] = panel[
                pl.ds(c * 4 * SB + n // 2 * SHARE, SHARE), pl.ds(n % 2 * LANES, LANES)
            ]


def overlap(weight, row, tiles, received):
    states = 2 * LANES
    return pl.pallas_call(
        functools.partial(overlap_kernel, weight),
        out_shape=jax.ShapeDtypeStruct((8 * tiles.shape[1], SHARE, LANES), F32),
        in_specs=[SM, ANY, VM],
        out_specs=VM,
        scratch_shapes=[pltpu.VMEM(tiles.shape[1:], F32)]
        + [pltpu.VMEM((states, states), F32)] * 3
        + [pltpu.SemaphoreType.DMA],
        compiler_params=PARAMS,
        cost_estimate=cost(5),
    )(row, tiles, received)


def place_kernel(moved, *refs):
    out_ref = refs[-1]
    for p in range(moved.shape[0] // 4):
        for y in range(2):
            for core in range(2):
                out_ref[pl.ds(y * 2 * SB, 2 * SB), pl.ds((2 * p + core) * NB, NB)] = moved[
                    p * 4 + y * 2 + core
                ]


def place(half, moved, *placed):
    steps, sources = 2, moved.shape[0]
    width = sources // 2 * NB // (2 * steps)
    return pl.pallas_call(
        place_kernel,
        out_shape=jax.ShapeDtypeStruct((4 * SB, sources // 2 * NB), F32),
        grid=(steps,),
        in_specs=[
            pl.BlockSpec(
                (sources // (2 * steps),) + moved.shape[1:], lambda i: (half * steps + i, 0, 0)
            )
        ] + [ANY] * len(placed),
        out_specs=pl.BlockSpec((4 * SB, width), lambda i: (0, half * steps + i)),
        input_output_aliases={1: 0} if placed else {},
        compiler_params=PARAMS,
        cost_estimate=cost(3),
    )(moved, *placed)


def shards(block, inv_sqrt_mass, potential, elem_scale, connectivity, elem_matrix):
    both = ("nodes", "grid")
    parts = lax.axis_size("nodes")
    grid = lax.axis_index("grid")
    row, core = grid // 2, grid % 2
    owned = 2 * HB

    def along(step):
        pairs = []
        for y in range(2):
            for source in range(2 * parts):
                target = source + step
                if 0 <= target < 2 * parts:
                    pairs.append((
                        source // 2 * 4 + y * 2 + source % 2,
                        target // 2 * 4 + y * 2 + target % 2,
                    ))
        return lambda value: lax.ppermute(value, both, pairs)

    to_previous, to_next = along(-1), along(1)

    other = lax.dynamic_slice(block, (0, (1 - core) * owned), (block.shape[0], owned))
    other = lax.ppermute(other, "grid", [(0, 1), (1, 0), (2, 3), (3, 2)])
    fields = jnp.stack([inv_sqrt_mass, potential]).reshape(2, -1, LANES)
    count = HB // LANES
    rim = lax.ppermute(fields[:, :count], "nodes", [(n, n - 1) for n in range(1, parts)])
    own = lax.dynamic_slice(fields, (0, core * 2 * count, 0), (2, 2 * count, LANES))
    m_l, w_l, m_u, w_u = spread(own[0], own[1])

    conn = lax.dynamic_slice(connectivity, (core * 2 * EL, 0), (2 * EL, NPE)) - core * owned
    conn = jnp.pad(conn, ((0, 0), (0, LANES - NPE)))
    c_l, c_u = conn[:EL].reshape(-1), (conn[EL:] - HB).reshape(-1)
    scale = lax.dynamic_slice(elem_scale, (core * 2 * EL,), (2 * EL,))
    s_l, s_u = scale[:EL], scale[EL:]
    matrix = jnp.pad(elem_matrix, ((0, LANES - NPE), (0, LANES - NPE)))

    u_l, u_u = enter(core[None], block, other, own[0])
    u_h = to_previous(u_l)
    a_l, rim = lax.optimization_barrier((u_l, rim))
    last = jnp.where(core == 0, fields[:, 2 * count:3 * count], rim)
    lo_a, hi_a = element_call(kernel_a, 2, 0, c_l, s_l, matrix, a_l, u_u)
    lo_a_next = to_previous(lo_a)
    m_h, w_h = spread(last[0], last[1])
    x_u, hi_b = element_call(kernel_b, 2, 3, c_u, s_u, matrix, u_u, u_h, hi_a, m_u, w_u)
    hi_b_previous = to_next(hi_b)
    lo_c, hi_c = element_call(
        kernel_c, 2, 5, c_u, s_u, matrix, x_u, hi_b, lo_a_next, u_h, m_h, w_h
    )
    hi_c_previous = to_next(hi_c)
    f_l, f_u = element_call(
        kernel_d, 2, 9, c_l, s_l, matrix,
        x_u, lo_a, hi_b_previous, u_l, m_l, w_l, lo_c, u_u, m_u, w_u, params=LARGE,
    )
    tiles, away = finish(row[None], f_l, hi_c_previous, m_l, f_u, own[0])
    across = [(0, 2), (1, 3), (2, 0), (3, 1)]
    late = lax.ppermute(away[count // 2:], "grid", across)
    early = lax.ppermute(away[:count // 2], "grid", across)
    tiles, early = lax.optimization_barrier((tiles, early))
    received = jnp.concatenate([early, late], axis=0)

    moved = lax.all_to_all(
        tiles.reshape(4 * parts, 2 * SB, NB), both, split_axis=0, concat_axis=0, tiled=True
    )
    shares = overlap(1.0 / (parts * 4 * HB), row[None], tiles, received)
    moved, shares = lax.optimization_barrier((moved, shares))
    shares = lax.all_to_all(shares, both, split_axis=0, concat_axis=0, tiled=True)
    cyclic = place(0, moved)
    share = jnp.sum(shares, axis=0)
    share, moved, cyclic = lax.optimization_barrier((share, moved, cyclic))
    shares = lax.all_to_all(
        jnp.broadcast_to(share[None], (parts, SHARE, LANES)),
        "nodes", split_axis=0, concat_axis=0, tiled=True,
    )
    cyclic = place(1, moved, cyclic)
    rows = shares.reshape(parts // 2, 2, SHARE, LANES).transpose(0, 2, 1, 3)
    intersection = rows.reshape(4 * SB, 2 * LANES).T
    return (cyclic, intersection)


def solution(mesh):
    placed = (P("grid", "nodes"), P("nodes"), P("nodes"), P("nodes"), P("nodes", None), P())
    return jax.shard_map(
        shards,
        mesh=mesh,
        in_specs=placed,
        out_specs=(P("grid", "nodes"), P(None, "grid")),
        check_vma=False,
    )
```

```python
import functools

import jax
import jax.numpy as jnp
from jax import lax
from jax.experimental import pallas as pl
from jax.experimental.pallas import tpu as pltpu
from jax.sharding import PartitionSpec as P

F32, BF16 = jnp.float32, jnp.bfloat16
HB = 2048
LANES = 128
NPE = 125
EL = 32
STRIDE = 64
GROUP = 8
NB, SB = 128, 16

LOWEST, CUT, TOP = -2.0, 4.0, 32.0
HALF = (TOP - CUT) / 2.0
CENTRE = (TOP + CUT) / 2.0
SIGMA = HALF / (LOWEST - CENTRE)
SIGMA_TWO = 1.0 / (2.0 / SIGMA - SIGMA)
A1 = SIGMA / HALF
A2 = 2.0 * SIGMA_TWO / HALF
A3 = SIGMA * SIGMA_TWO

VM = pl.BlockSpec(memory_space=pltpu.VMEM)
SM = pl.BlockSpec(memory_space=pltpu.SMEM)
ANY = pl.BlockSpec(memory_space=pl.ANY)
NODE_BLOCK = jax.ShapeDtypeStruct((HB, LANES), F32)
PARAMS = pltpu.CompilerParams(vmem_limit_bytes=40 << 20)
LARGE = pltpu.CompilerParams(vmem_limit_bytes=56 << 20)
SHARE = 4


def split(value):
    high = value.astype(BF16)
    return high, (value - high.astype(F32)).astype(BF16)


def dot(a, b):
    return lax.dot_general(a, b, (((1,), (0,)), ((), ())), preferred_element_type=F32)


def dot_t(a, b):
    return lax.dot_general(a, b, (((1,), (1,)), ((), ())), preferred_element_type=F32)


def cost(microseconds):
    return pl.CostEstimate(flops=0, transcendentals=0, bytes_accessed=int(microseconds * 3.0e6))


RUN = EL // GROUP
REACH = 2304
PIECE = 256


def clear(sums):
    for k, ref in enumerate(sums):
        start = k * RUN * STRIDE
        size = min(REACH, 2 * HB - start)
        ref[pl.ds(start, size), :] = jnp.zeros((size, LANES), F32)


def add_elements(conn, scale, matrix, values, picked, local, sums):
    high, low = split(matrix[...])
    left = jnp.concatenate(
        [
            jnp.concatenate([high, high], axis=1),
            jnp.concatenate([low, jnp.zeros_like(low)], axis=1),
        ],
        axis=0,
    )
    for ref in picked:
        ref[pl.ds(NPE, LANES - NPE), :] = jnp.zeros((LANES - NPE, LANES), F32)

    @pl.loop(0, RUN)
    def _(step):
        base = step * LANES
        for i in range(NPE):
            for k in range(GROUP):
                node = conn[base + (k * RUN * LANES + i)]
                picked[k][pl.ds(i, 1), :] = values[pl.ds(node, 1), :]
        for k in range(0, GROUP, 2):
            pair = [split(picked[k + j][...]) for j in range(2)]
            right = jnp.concatenate(
                [
                    jnp.concatenate([pair[0][0], pair[1][0]], axis=1),
                    jnp.concatenate([pair[0][1], pair[1][1]], axis=1),
                ],
                axis=0,
            )
            product = dot(left, right)
            product = product[:LANES] + product[LANES:]
            for j in range(2):
                local[k + j][...] = (
                    product[:, j * LANES:(j + 1) * LANES] * scale[step + (k + j) * RUN]
                )
        for i in range(NPE):
            for k in range(GROUP):
                node = conn[base + (k * RUN * LANES + i)]
                row = pl.ds(node, 1)
                sums[k][row, :] = sums[k][row, :] + local[k][pl.ds(i, 1), :]


def total(sums, start):
    pieces = []
    for row in range(start, start + HB, PIECE):
        parts = [
            ref[pl.ds(row, PIECE), :]
            for k, ref in enumerate(sums)
            if 0 <= row - k * RUN * STRIDE < REACH
        ]
        while len(parts) > 1:
            parts = [a + b for a, b in zip(parts[::2], parts[1::2])] + (
                [parts[-1]] if len(parts) % 2 else []
            )
        pieces.append(parts[0])
    return jnp.concatenate(pieces, axis=0)


def fetch(pairs, sems):
    copies = [
        pltpu.make_async_copy(source, target, sems.at[i])
        for i, (source, target) in enumerate(pairs)
    ]
    for copy in copies:
        copy.start()
    return copies


LOW, HIGH = pl.ds(0, HB), pl.ds(HB, HB)


def kernel_a(conn, scale, matrix, u_l, u_u, low_ref, high_ref, sems, values, *scratch):
    picked, local, sums = scratch[:GROUP], scratch[GROUP:2 * GROUP], scratch[2 * GROUP:]
    copies = fetch([(u_l, values.at[LOW]), (u_u, values.at[HIGH])], sems)
    clear(sums)
    for copy in copies:
        copy.wait()
    add_elements(conn, scale, matrix, values, picked, local, sums)
    low_ref[...] = total(sums, 0)
    high_ref[...] = total(sums, HB)


def kernel_b(conn, scale, matrix, u_u, u_h, hi_a, m_u, w_u, x_ref, high_ref,
             sems, values, t0, t1, t2, *scratch):
    picked, local, sums = scratch[:GROUP], scratch[GROUP:2 * GROUP], scratch[2 * GROUP:]
    copies = fetch(
        [(u_u, values.at[LOW]), (u_h, values.at[HIGH]), (hi_a, t0), (m_u, t1), (w_u, t2)], sems
    )
    clear(sums)
    for copy in copies:
        copy.wait()
    add_elements(conn, scale, matrix, values, picked, local, sums)
    x_ref[...] = A1 * (t1[...] * (t0[...] + total(sums, 0)) + t2[...] * values[LOW, :])
    high_ref[...] = total(sums, HB)


def kernel_c(conn, scale, matrix, x_u, hi_b, lo_a, u_h, m_h, w_h, low_ref, high_ref,
             sems, values, t0, t1, t2, t3, t4, *scratch):
    picked, local, sums = scratch[:GROUP], scratch[GROUP:2 * GROUP], scratch[2 * GROUP:]
    copies = fetch(
        [(x_u, values.at[LOW]), (hi_b, t0), (lo_a, t1), (u_h, t2), (m_h, t3), (w_h, t4)], sems
    )
    clear(sums)
    for copy in copies:
        copy.wait()
    values[HIGH, :] = A1 * (t3[...] * (t0[...] + t1[...]) + t4[...] * t2[...])
    add_elements(conn, scale, matrix, values, picked, local, sums)
    low_ref[...] = total(sums, 0)
    high_ref[...] = total(sums, HB)


def kernel_d(conn, scale, matrix, x_u, lo_a, hi_b, u_l, m_l, w_l, lo_c, u_u, m_u, w_u,
             low_ref, high_ref, sems, values, t0, t1, t2, t3, t4, t5, t6, t7, t8, *scratch):
    picked, local, sums = scratch[:GROUP], scratch[GROUP:2 * GROUP], scratch[2 * GROUP:]
    copies = fetch(
        [(x_u, values.at[HIGH]), (lo_a, t0), (hi_b, t1), (u_l, t2), (m_l, t3), (w_l, t4),
         (lo_c, t5), (u_u, t6), (m_u, t7), (w_u, t8)],
        sems,
    )
    clear(sums)
    for copy in copies[:6]:
        copy.wait()
    values[LOW, :] = A1 * (t3[...] * (t0[...] + t1[...]) + t4[...] * t2[...])
    add_elements(conn, scale, matrix, values, picked, local, sums)
    for copy in copies[6:]:
        copy.wait()
    low_ref[...] = A2 * (t3[...] * total(sums, 0) + t4[...] * values[LOW, :]) - A3 * t2[...]
    high_ref[...] = (
        A2 * (t7[...] * (t5[...] + total(sums, HB)) + t8[...] * values[HIGH, :]) - A3 * t6[...]
    )


def element_call(kernel, outs, temporaries, *operands, params=PARAMS):
    count = len(operands) - 3
    return pl.pallas_call(
        kernel,
        out_shape=(NODE_BLOCK,) * outs,
        in_specs=[SM, SM, VM] + [ANY] * count,
        out_specs=(VM,) * outs,
        scratch_shapes=[pltpu.SemaphoreType.DMA((count,)), pltpu.VMEM((2 * HB, LANES), F32)]
        + [pltpu.VMEM((HB, LANES), F32)] * temporaries
        + [pltpu.VMEM((LANES, LANES), F32)] * (2 * GROUP)
        + [pltpu.VMEM((2 * HB, LANES), F32)] * GROUP,
        compiler_params=params,
        cost_estimate=cost(13),
    )(*operands)


def spread_kernel(mass, well, *outs):
    count = HB // LANES
    for chunk in range(mass.shape[0]):
        rows = pl.ds(chunk % count * LANES, LANES)
        one = jnp.broadcast_to(mass[pl.ds(chunk, 1), :], (LANES, LANES))
        outs[chunk // count * 2][rows, :] = (one * one).T
        two = jnp.broadcast_to(well[pl.ds(chunk, 1), :] - CENTRE, (LANES, LANES))
        outs[chunk // count * 2 + 1][rows, :] = two.T


def spread(mass, well):
    outs = 2 * (mass.shape[0] * LANES // HB)
    return pl.pallas_call(
        spread_kernel,
        out_shape=(NODE_BLOCK,) * outs,
        in_specs=[VM, VM],
        out_specs=(VM,) * outs,
        compiler_params=PARAMS,
        cost_estimate=cost(outs),
    )(mass, well)


def enter_kernel(core, block, other, mass, low_ref, high_ref, mine, sem):
    owned = 2 * HB
    start = pl.multiple_of(core[0] * owned, owned)
    copy = pltpu.make_async_copy(block.at[:, pl.ds(start, owned)], mine, sem)
    copy.start()
    copy.wait()
    first = core[0] == 0
    for chunk in range(owned // LANES):
        columns = pl.ds(chunk * LANES, LANES)
        a, b = mine[:, columns], other[:, columns]
        stacked = jnp.concatenate([jnp.where(first, a, b), jnp.where(first, b, a)], axis=0)
        target = low_ref if chunk < HB // LANES else high_ref
        rows = pl.ds(chunk % (HB // LANES) * LANES, LANES)
        target[rows, :] = (stacked * mass[pl.ds(chunk, 1), :]).T


def enter(core, block, other, mass):
    return pl.pallas_call(
        enter_kernel,
        out_shape=(NODE_BLOCK, NODE_BLOCK),
        in_specs=[SM, ANY, VM, VM],
        out_specs=(VM, VM),
        scratch_shapes=[pltpu.VMEM((block.shape[0], 2 * HB), F32), pltpu.SemaphoreType.DMA],
        compiler_params=PARAMS,
        cost_estimate=cost(4),
    )(core, block, other, mass)


FINISH = 512


def finish_kernel(row, f_l, hi_c, m_l, f_u, mass, out_ref, away_ref):
    step = pl.program_id(0)
    count = FINISH // LANES
    for chunk in range(count):
        rows = pl.ds(chunk * LANES, LANES)
        turned = []
        for half in range(2):
            value = f_l[rows, :] + A2 * (m_l[rows, :] * hi_c[rows, :]) if half == 0 else f_u[rows, :]
            at = half * (HB // LANES) + step * count + chunk
            value = value.T / mass[pl.ds(at, 1), :]
            order = [
                value[kk * 4 * SB + c * SB:kk * 4 * SB + (c + 1) * SB, :]
                for c in range(4) for kk in range(2)
            ]
            value = jnp.concatenate(order, axis=0)
            turned.append(value)
            out_ref[half, chunk] = value
        away_ref[chunk] = jnp.where(row[0] == 0, turned[1], turned[0])


def finish(row, *operands):
    part = pl.BlockSpec((FINISH, LANES), lambda i: (i, 0))
    count = FINISH // LANES
    return pl.pallas_call(
        finish_kernel,
        out_shape=(
            jax.ShapeDtypeStruct((2, HB // LANES, LANES, LANES), F32),
            jax.ShapeDtypeStruct((HB // LANES, LANES, LANES), F32),
        ),
        grid=(HB // FINISH,),
        in_specs=[SM] + [part] * (len(operands) - 1) + [VM],
        out_specs=(
            pl.BlockSpec((2, count, LANES, LANES), lambda i: (0, i, 0, 0)),
            pl.BlockSpec((count, LANES, LANES), lambda i: (i, 0, 0)),
        ),
        compiler_params=LARGE,
        cost_estimate=cost(3),
    )(row, *operands)


def overlap_kernel(weight, row, tiles, received, shares, mine, main, cross, panel, sem):
    copy = pltpu.make_async_copy(tiles.at[row[0]], mine, sem)
    copy.start()
    main[...] = jnp.zeros_like(main)
    cross[...] = jnp.zeros_like(cross)
    first = row[0] == 0
    copy.wait()

    @pl.loop(0, received.shape[0] // 2)
    def _(step):
        blocks = []
        for c in range(4):
            rows = pl.ds(c * 2 * SB, 2 * SB)
            a = jnp.concatenate([mine[2 * step, rows, :], mine[2 * step + 1, rows, :]], axis=1)
            b = jnp.concatenate(
                [received[2 * step, rows, :], received[2 * step + 1, rows, :]], axis=1
            )
            blocks += [jnp.where(first, a, b), jnp.where(first, b, a)]
        high, low = split(jnp.concatenate(blocks, axis=0))
        main[...] += dot_t(high, high)
        cross[...] += dot_t(high, low)

    panel[...] = (main[...] + (cross[...] + cross[...].T)) * weight
    for n in range(4 * SB // SHARE * 2):
        for c in range(4):
            shares[n * 4 + c] = panel[
                pl.ds(c * 4 * SB + n // 2 * SHARE, SHARE), pl.ds(n % 2 * LANES, LANES)
            ]


def overlap(weight, row, tiles, received):
    states = 2 * LANES
    return pl.pallas_call(
        functools.partial(overlap_kernel, weight),
        out_shape=jax.ShapeDtypeStruct((8 * tiles.shape[1], SHARE, LANES), F32),
        in_specs=[SM, ANY, VM],
        out_specs=VM,
        scratch_shapes=[pltpu.VMEM(tiles.shape[1:], F32)]
        + [pltpu.VMEM((states, states), F32)] * 3
        + [pltpu.SemaphoreType.DMA],
        compiler_params=PARAMS,
        cost_estimate=cost(5),
    )(row, tiles, received)


def place_kernel(moved, *refs):
    out_ref = refs[-1]
    for p in range(moved.shape[0] // 4):
        for y in range(2):
            for core in range(2):
                out_ref[pl.ds(y * 2 * SB, 2 * SB), pl.ds((2 * p + core) * NB, NB)] = moved[
                    p * 4 + y * 2 + core
                ]


def place(half, moved, *placed):
    steps, sources = 2, moved.shape[0]
    width = sources // 2 * NB // (2 * steps)
    return pl.pallas_call(
        place_kernel,
        out_shape=jax.ShapeDtypeStruct((4 * SB, sources // 2 * NB), F32),
        grid=(steps,),
        in_specs=[
            pl.BlockSpec(
                (sources // (2 * steps),) + moved.shape[1:], lambda i: (half * steps + i, 0, 0)
            )
        ] + [ANY] * len(placed),
        out_specs=pl.BlockSpec((4 * SB, width), lambda i: (0, half * steps + i)),
        input_output_aliases={1: 0} if placed else {},
        compiler_params=PARAMS,
        cost_estimate=cost(3),
    )(moved, *placed)


def shards(block, inv_sqrt_mass, potential, elem_scale, connectivity, elem_matrix):
    both = ("nodes", "grid")
    parts = lax.axis_size("nodes")
    grid = lax.axis_index("grid")
    row, core = grid // 2, grid % 2
    owned = 2 * HB

    def along(step):
        pairs = []
        for y in range(2):
            for source in range(2 * parts):
                target = source + step
                if 0 <= target < 2 * parts:
                    pairs.append((
                        source // 2 * 4 + y * 2 + source % 2,
                        target // 2 * 4 + y * 2 + target % 2,
                    ))
        return lambda value: lax.ppermute(value, both, pairs)

    to_previous, to_next = along(-1), along(1)

    other = lax.dynamic_slice(block, (0, (1 - core) * owned), (block.shape[0], owned))
    other = lax.ppermute(other, "grid", [(0, 1), (1, 0), (2, 3), (3, 2)])
    fields = jnp.stack([inv_sqrt_mass, potential]).reshape(2, -1, LANES)
    count = HB // LANES
    rim = lax.ppermute(fields[:, :count], "nodes", [(n, n - 1) for n in range(1, parts)])
    own = lax.dynamic_slice(fields, (0, core * 2 * count, 0), (2, 2 * count, LANES))
    m_l, w_l, m_u, w_u = spread(own[0], own[1])

    conn = lax.dynamic_slice(connectivity, (core * 2 * EL, 0), (2 * EL, NPE)) - core * owned
    conn = jnp.pad(conn, ((0, 0), (0, LANES - NPE)))
    c_l, c_u = conn[:EL].reshape(-1), (conn[EL:] - HB).reshape(-1)
    scale = lax.dynamic_slice(elem_scale, (core * 2 * EL,), (2 * EL,))
    s_l, s_u = scale[:EL], scale[EL:]
    matrix = jnp.pad(elem_matrix, ((0, LANES - NPE), (0, LANES - NPE)))

    u_l, u_u = enter(core[None], block, other, own[0])
    u_h = to_previous(u_l)
    a_l, rim = lax.optimization_barrier((u_l, rim))
    last = jnp.where(core == 0, fields[:, 2 * count:3 * count], rim)
    lo_a, hi_a = element_call(kernel_a, 2, 0, c_l, s_l, matrix, a_l, u_u)
    lo_a_next = to_previous(lo_a)
    m_h, w_h = spread(last[0], last[1])
    x_u, hi_b = element_call(kernel_b, 2, 3, c_u, s_u, matrix, u_u, u_h, hi_a, m_u, w_u)
    hi_b_previous = to_next(hi_b)
    lo_c, hi_c = element_call(
        kernel_c, 2, 5, c_u, s_u, matrix, x_u, hi_b, lo_a_next, u_h, m_h, w_h
    )
    hi_c_previous = to_next(hi_c)
    f_l, f_u = element_call(
        kernel_d, 2, 9, c_l, s_l, matrix,
        x_u, lo_a, hi_b_previous, u_l, m_l, w_l, lo_c, u_u, m_u, w_u, params=LARGE,
    )
    tiles, away = finish(row[None], f_l, hi_c_previous, m_l, f_u, own[0])
    received = lax.ppermute(away, "grid", [(0, 2), (1, 3), (2, 0), (3, 1)])

    moved = lax.all_to_all(
        tiles.reshape(4 * parts, 2 * SB, NB), both, split_axis=0, concat_axis=0, tiled=True
    )
    shares = overlap(1.0 / (parts * 4 * HB), row[None], tiles, received)
    moved, shares = lax.optimization_barrier((moved, shares))
    shares = lax.all_to_all(shares, both, split_axis=0, concat_axis=0, tiled=True)
    cyclic = place(0, moved)
    share = jnp.sum(shares, axis=0)
    share, moved, cyclic = lax.optimization_barrier((share, moved, cyclic))
    shares = lax.all_to_all(
        jnp.broadcast_to(share[None], (parts, SHARE, LANES)),
        "nodes", split_axis=0, concat_axis=0, tiled=True,
    )
    cyclic = place(1, moved, cyclic)
    rows = shares.reshape(parts // 2, 2, SHARE, LANES).transpose(0, 2, 1, 3)
    intersection = rows.reshape(4 * SB, 2 * LANES).T
    return (cyclic, intersection)


def solution(mesh):
    placed = (P("grid", "nodes"), P("nodes"), P("nodes"), P("nodes"), P("nodes", None), P())
    return jax.shard_map(
        shards,
        mesh=mesh,
        in_specs=placed,
        out_specs=(P("grid", "nodes"), P(None, "grid")),
        check_vma=False,
    )
```
